32 devices in a mesh: seq: 4 (over z), head: 8 (over y, x, core).
Axes of the slice: x: 2, y: 2, z: 4, core: 2. Of those that a mesh axis runs over, the one named last changes fastest.
Arguments:
- query: float32 [3072, 1024], P('seq', 'head'), may hold values from -6 to 6
- key_in: float32 [3072, 1024], P('seq', 'head'), may hold values from -6 to 6
- value: float32 [3072, 1024], P('seq', 'head'), may hold values from -6 to 6
- out_grad: float32 [3072, 1024], P('seq', 'head'), may hold values from -6 to 6
- head_scale: float32 [8], P('head'), may hold values from 0.5 to 2
- norm_gain: float32 [1024], P('head'), may hold values from 0.5 to 1.5
- group_counts: int32 [4], replicated, may hold values from 1 to 6, 12 in all
Outputs:
- normed: float32 [3072, 1024], P('seq', 'head')
- grad_query: float32 [3072, 1024], P('seq', 'head')
- grad_key: float32 [3072, 1024], P('seq', 'head')
- grad_value: float32 [3072, 1024], P('seq', 'head')
The draws below stay inside these ranges and needn't reach their ends.
Inputs may be any that keep to these rules, and one draw needn't show every extreme that they name: The live rows of shard i are its first 128 * group_counts[i] rows; the counts sum to 3 * 4 and the largest is exactly 6.
All inputs are finite; a program needn't handle non-finite values.
Results may differ from the reference program's by a relative error of at most 0.0001.
Values sent between devices are 32-bit elements; how exact they have to be, the bound alone decides.
A program may use at most 64 MiB of HBM per device.

```python
import math
import jax
import jax.numpy as jnp
import numpy as np
from jax import lax

DH = 128
HEADS = 8
GROUP = 128
MEAN_GROUPS = 3
CAP = 768
SEQ_BUF = 3072
WIDTH = 1024
N_SEQ = 4


def shard_levels(stream_key, extent, split, low, largest):
    loudness = 1.0
    for dim, parts in split:
        draws = jax.random.uniform(jax.random.fold_in(jax.random.fold_in(stream_key, 6), dim), (parts,), jnp.float32, low / len(split), largest / len(split))
        loudness = loudness * jnp.repeat(jnp.exp(draws), extent[dim] // parts).reshape((-1,) + (1,) * (len(extent) - 1 - dim))
    return loudness


def length_profile(amount, total, most, lean):
    weights = [(1 << 20) // math.isqrt(grade ** lean) + 1 for grade in range(2, amount + 1)]
    rest, holding = total - most - (amount - 1), [1] * (amount - 1)
    while rest > 0:
        free = [i for i in range(amount - 1) if holding[i] < most]
        pool, remaining = sum([weights[i] for i in free]), rest
        for i in free:
            more = min(most - holding[i], max(1, remaining * weights[i] // pool), rest)
            holding[i] = holding[i] + more
            rest = rest - more
    return np.array([most] + holding)


def ragged_sizes(own_key, count, total, most, lean):
    if count == 2:
        one = jax.random.randint(own_key, (), max(1, total - most), min(most, total - 1) + 1)
        return jnp.stack([one, total - one])
    sizes = jnp.asarray(length_profile(count, total, most, lean), jnp.int32)
    couples = (count - 1) // 2
    giver, sink = sizes[1:1 + 2 * couples:2], sizes[2:2 + 2 * couples:2]
    room = jnp.minimum(giver - 1, most - sink)
    passed = jax.random.randint(jax.random.fold_in(own_key, 1), (couples,), 0, 1 << 20) % (room + 1)
    sizes = sizes.at[1:1 + 2 * couples:2].set(giver - passed).at[2:2 + 2 * couples:2].set(sink + passed)
    return sizes[jax.random.permutation(jax.random.fold_in(own_key, 2), count)]


def noise(key, shape, spread, limit, cuts=(), kind=jnp.bfloat16):
    result = spread * jax.random.normal(key, shape, jnp.float32)
    if cuts:
        result = result * shard_levels(key, shape, cuts, -0.22, 0.18)
    return jnp.clip(result, -limit, limit).astype(kind)


def setup_inputs(seed: int = 0) -> dict:
    key_of = jax.random.split(jax.random.key(seed), 8)
    query = noise(key_of[0], (SEQ_BUF, WIDTH), 1.0, 6.0, ((0, 4), (1, 8)), jnp.float32)
    key_in = noise(key_of[1], (SEQ_BUF, WIDTH), 1.0, 6.0, ((0, 4), (1, 8)), jnp.float32)
    value = noise(key_of[2], (SEQ_BUF, WIDTH), 1.0, 6.0, ((0, 4), (1, 8)), jnp.float32)
    out_grad = noise(key_of[3], (SEQ_BUF, WIDTH), 1.0, 6.0, ((0, 4), (1, 8)), jnp.float32)
    head_scale = jnp.clip(jnp.exp(math.log(2.0) - 1.3862944 * jax.random.uniform(key_of[4], (HEADS,), jnp.float32) ** shard_levels(key_of[4], (HEADS,), ((0, 8),), -0.2, 0.2)), 0.5, 2.0)
    norm_gain = jnp.clip(1.0 + 0.1 * jax.random.normal(key_of[5], (WIDTH,), jnp.float32), 0.5, 1.5)
    group_counts = ragged_sizes(key_of[6], N_SEQ, MEAN_GROUPS * N_SEQ, 2 * MEAN_GROUPS, 2).astype(jnp.int32)
    return dict(query=query, key_in=key_in, value=value, out_grad=out_grad, head_scale=head_scale, norm_gain=norm_gain, group_counts=group_counts)


def reference(query, key_in, value, out_grad, head_scale, norm_gain, group_counts):
    row_ids = jnp.arange(SEQ_BUF)
    shard_ids = row_ids // CAP
    live_rows = (row_ids - shard_ids * CAP < group_counts[shard_ids] * GROUP)[:, None]
    causal = jnp.tril(jnp.ones((GROUP, GROUP), dtype=bool))
    highest = lax.Precision.HIGHEST

    def forward_layer(q_all, k_all, v_all):
        blocks = tuple((jnp.where(live_rows, source, 0.0).reshape(SEQ_BUF // GROUP, GROUP, HEADS, DH) for source in (q_all, k_all, v_all)))

        def advance(running, block_items):
            q_block, k_block, v_block = block_items
            scores = jnp.einsum('thd,shd->hts', q_block, k_block, precision=highest)
            scores = jnp.where(causal[None], scores, 0.0)
            local_part = jnp.einsum('hts,shd->thd', scores, v_block, precision=highest)
            carried = jnp.einsum('thd,hde->the', q_block, running, precision=highest)
            running = running + jnp.einsum('shd,she->hde', k_block, v_block, precision=highest)
            return (running, local_part + carried)
        start_state = jnp.zeros((HEADS, DH, DH), jnp.float32)
        _, attended = lax.scan(advance, start_state, blocks)
        attended = attended.reshape(SEQ_BUF, HEADS, DH) * head_scale[None, :, None]
        scaled = attended.reshape(SEQ_BUF, WIDTH)
        inverse = lax.rsqrt(lax.optimization_barrier(jnp.mean(scaled * scaled, axis=1, keepdims=True)) + 1e-05)
        return scaled * inverse * norm_gain[None, :]
    normed, pullback = jax.vjp(forward_layer, query, key_in, value)
    grad_query, grad_key, grad_value = pullback(out_grad)
    return (normed, grad_query, grad_key, grad_value)
```

```python
import functools

import jax
import jax.numpy as jnp
from jax import lax
from jax.experimental import pallas as pl
from jax.experimental.pallas import tpu as pltpu
from jax.sharding import PartitionSpec as P

GROUP = 128
EPS = 1e-05
F32 = jnp.float32
BF16 = jnp.bfloat16
MESH = pl.DeviceIdType.MESH
NN = (((1,), (0,)), ((), ()))
NT = (((1,), (1,)), ((), ()))
TN = (((0,), (0,)), ((), ()))


def dot(left, right, dims):
    return lax.dot_general(left, right, dims, preferred_element_type=F32)


def split(x):
    high = x.astype(BF16)
    low = (x - high.astype(F32)).astype(BF16)
    return high, low


def beside(pair):
    return jnp.concatenate(pair, axis=1)


def add_rows(x):
    half = x.shape[0] // 2
    return x[:half] + x[half:]


def add_columns(x):
    half = x.shape[1] // 2
    return x[:, :half] + x[:, half:]


def stacked(s):
    top = jnp.concatenate([s[0], s[0]], axis=1)
    bottom = jnp.concatenate([s[1], jnp.zeros_like(s[1])], axis=1)
    return jnp.concatenate([top, bottom], axis=0)


def rows_by_rows(a, b):
    left = jnp.concatenate([a[0], a[1], a[0]], axis=1)
    right = jnp.concatenate([b[0], b[0], b[1]], axis=1)
    return dot(left, right, NT)


def rows_by_columns(a, b):
    left = jnp.concatenate([a[0], a[1], a[0]], axis=1)
    right = jnp.concatenate([b[0], b[0], b[1]], axis=0)
    return dot(left, right, NN)


def times(a, b):
    return add_columns(dot(a[0], beside(b), NN)) + dot(a[1], b[0], NN)


def columns_times(a, b):
    return add_columns(dot(a[0], beside(b), TN)) + dot(a[1], b[0], TN)


def times_state(a, s):
    top = jnp.concatenate([s[0], s[1]], axis=1)
    bottom = jnp.concatenate([s[0], jnp.zeros_like(s[0])], axis=1)
    return add_columns(dot(beside(a), jnp.concatenate([top, bottom], axis=0), NN))


def times_state_t(a, s):
    return add_columns(dot(beside(a), stacked(s), NT))


def state_by_rows(s, a):
    return add_rows(dot(s, beside(a), NT))


def outer(a, b):
    return add_rows(add_columns(dot(beside(a), beside(b), TN)))


def kernel(
    n_seq, n_head, block, head_scale, counts_hbm,
    q_hbm, k_hbm, v_hbm, g_hbm, gain_hbm,
    normed, gq, gk, gv, k_h, k_l, v_h, v_l, t_out,
    counts, q_in, k_in, v_in, g_in, gain,
    q_h, q_l, p_h, p_l, mine_t, gg_t, o_h, o_l,
    send_s, recv_s, send_t, recv_t, sums, sums_in,
    in_sem, s_send, s_recv, t_send, t_recv, h_send, h_recv,
):
    cap, d = q_in.shape
    blocks = cap // block
    per = block // GROUP
    pos = lax.axis_index("seq")
    head = lax.axis_index("head")
    half = sums.shape[0] // 2

    barrier = pltpu.get_barrier_semaphore()
    for step in range(1, n_seq):
        pl.semaphore_signal(barrier, inc=1, device_id={"seq": lax.rem(pos + step, n_seq)}, device_id_type=MESH)
    loads = [
        pltpu.make_async_copy(src, dst, in_sem.at[i])
        for i, (src, dst) in enumerate(
            (
                (counts_hbm, counts), (k_hbm, k_in), (v_hbm, v_in), (q_hbm, q_in),
                (g_hbm, g_in), (gain_hbm, gain),
            )
        )
    ]
    for load in loads:
        load.start()
    for step in range(1, n_head):
        pl.semaphore_signal(barrier, inc=1, device_id={"head": lax.rem(head + step, n_head)}, device_id_type=MESH)

    def exchange(way, src, dst, s_sem, r_sem):
        order = pos if way == 1 else n_seq - 1 - pos
        to_last = n_seq - 1 - order

        def message(reach):
            return pltpu.make_async_remote_copy(
                src_ref=src, dst_ref=dst.at[reach - 1],
                send_sem=s_sem.at[reach - 1], recv_sem=r_sem.at[reach - 1],
                device_id={"seq": pos + way * reach}, device_id_type=MESH,
            )

        def clear():
            for reach in range(1, n_seq):

                @pl.when(order < reach)
                def _():
                    dst[reach - 1] = jnp.zeros(dst.shape[1:], F32)

        def start(reach=None):
            if reach is None:

                @pl.when(to_last > 0)
                def _():
                    message(to_last).start()

            else:

                @pl.when(reach < to_last)
                def _():
                    message(reach).start()

        def carried():
            total = None
            for reach in range(1, n_seq):

                @pl.when(order >= reach)
                def _():
                    message(reach).wait_recv()

            for reach in range(1, n_seq):
                total = dst[reach - 1] if total is None else total + dst[reach - 1]
            return total

        def close():
            for reach in range(1, n_seq):

                @pl.when(reach <= to_last)
                def _():
                    message(reach).wait_send()

        return clear, start, carried, close

    s_clear, s_start, s_carried, s_close = exchange(1, send_s, recv_s, s_send, s_recv)
    t_clear, t_start, t_carried, t_close = exchange(-1, send_t, recv_t, t_send, t_recv)
    s_clear()
    t_clear()
    sums[...] = jnp.zeros_like(sums)

    row = lax.broadcasted_iota(jnp.int32, (block, d), 0)
    token = lax.broadcasted_iota(jnp.int32, (d, block), 1)
    upper = lax.broadcasted_iota(jnp.int32, (block, block), 0) <= lax.broadcasted_iota(jnp.int32, (block, block), 1)

    def take(b):
        return pl.ds(b * block, block)

    def pair(high, low, b):
        return high[take(b), :], low[take(b), :]

    loads[0].wait()
    live = counts[pos] * GROUP

    def keep(source, high, low, b):
        x = jnp.where(row + b * block < live, source[take(b), :], 0.0)
        high[take(b), :], low[take(b), :] = split(x)

    loads[1].wait()
    loads[2].wait()
    before = [jnp.zeros((d, d), F32)]
    for b in range(blocks):
        keep(k_in, k_h, k_l, b)
        keep(v_in, v_h, v_l, b)
        before.append(before[-1] + outer(pair(v_h, v_l, b), pair(k_h, k_l, b)))
    send_s[...] = before[-1]
    pl.semaphore_wait(barrier, n_head - 1 + n_seq - 1)
    s_start()

    loads[3].wait()
    loads[4].wait()
    loads[5].wait()
    scale = head_scale[0]
    gains = gain[...].reshape(1, d)
    for b in range(blocks):
        keep(q_in, q_h, q_l, b)
        q_b, k_b, v_b = pair(q_h, q_l, b), pair(k_h, k_l, b), pair(v_h, v_l, b)
        scores_t = split(jnp.where(upper, rows_by_rows(k_b, q_b), 0.0))
        p_h[take(b), :], p_l[take(b), :] = scores_t
        local = add_rows(dot(beside(v_b), scores_t[0], TN)) + dot(v_b[0], scores_t[1], TN)
        if b:
            local = local + state_by_rows(stacked(split(before[b])), q_b)
        mine_t[:, take(b)] = local
        gg_t[:, take(b)] = jnp.transpose(g_in[take(b), :] * gains)
        for reach in range(1, n_seq - 1):
            if b == min(2 * reach - 2, blocks - 1):
                s_start(reach)

    s_in = s_carried()
    arrived = stacked(split(s_in))
    for b in range(blocks):
        mine = (mine_t[:, take(b)] + state_by_rows(arrived, pair(q_h, q_l, b))) * scale
        mine_t[:, take(b)] = mine
        square = jnp.sum(mine * mine, axis=0, keepdims=True)
        cross = jnp.sum(gg_t[:, take(b)] * mine, axis=0, keepdims=True)
        for j in range(per):
            r = b * per + j
            sums[r : r + 1, :] = square[:, j * GROUP : (j + 1) * GROUP]
            sums[half + r : half + r + 1, :] = cross[:, j * GROUP : (j + 1) * GROUP]

    shares = [
        pltpu.make_async_remote_copy(
            src_ref=sums, dst_ref=sums_in.at[step - 1],
            send_sem=h_send.at[step - 1], recv_sem=h_recv.at[step - 1],
            device_id={"head": lax.rem(head + step, n_head)},
            device_id_type=MESH,
        )
        for step in range(1, n_head)
    ]
    for share in shares:
        share.start()
    total = sums[...]
    for share in shares:
        share.wait_recv()
    for step in range(1, n_head):
        total = total + sums_in[step - 1]
    features = d * n_head
    inverse = lax.rsqrt(total[:half] / features + EPS)
    factor = inverse * inverse * inverse * total[half:] / features

    def along(x, b):
        return jnp.concatenate([x[b * per + j : b * per + j + 1, :] for j in range(per)], axis=1)

    t_states = []
    for b in range(blocks):
        inv, fac = along(inverse, b), along(factor, b)
        grad = (gg_t[:, take(b)] * inv - mine_t[:, take(b)] * fac) * scale
        grad = split(jnp.where(token + b * block < live, grad, 0.0))
        o_h[:, take(b)], o_l[:, take(b)] = grad
        both = dot(jnp.concatenate(grad, axis=0), beside(pair(q_h, q_l, b)), NN)
        t_states.append(add_rows(add_columns(both)))
    after = [jnp.zeros((d, d), F32)]
    for b in range(blocks - 1, -1, -1):
        after.append(after[-1] + t_states[b])
    after = after[::-1]
    send_t[...] = after[0]
    t_start()

    for b in range(blocks):
        q_b, k_b, v_b = pair(q_h, q_l, b), pair(k_h, k_l, b), pair(v_h, v_l, b)
        o_t = o_h[:, take(b)], o_l[:, take(b)]
        o_b = jnp.transpose(o_t[0]), jnp.transpose(o_t[1])
        normed[take(b), :] = jnp.transpose(mine_t[:, take(b)] * along(inverse, b)) * gains
        pulled_t = split(jnp.where(upper, rows_by_columns(v_b, o_t), 0.0))
        gq[take(b), :] = times_state(o_b, split(s_in + before[b])) + columns_times(pulled_t, k_b)
        later = split(after[b + 1])
        gk[take(b), :] = times(pulled_t, q_b) + times_state(v_b, later)
        gv[take(b), :] = times(pair(p_h, p_l, b), o_b) + times_state_t(k_b, later)
        for reach in range(1, n_seq - 1):
            if b == blocks - 1:
                t_start(reach)

    t_out[...] = t_carried()
    s_close()
    for share in shares:
        share.wait_send()
    t_close()


def finish(
    block, normed, gq, gk, gv, k_h, k_l, v_h, v_l, t_in,
    normed_hbm, gq_hbm, gk_hbm, gv_hbm, gk_all, gv_all, sem,
):
    blocks = gk.shape[0] // block
    stores = [
        pltpu.make_async_copy(normed, normed_hbm, sem.at[2 * blocks]),
        pltpu.make_async_copy(gq, gq_hbm, sem.at[2 * blocks + 1]),
    ]
    for store in stores:
        store.start()
    state = split(t_in[...])
    for b in range(blocks):
        rows = pl.ds(b * block, block)
        gk_all[rows, :] = gk[rows, :] + times_state((v_h[rows, :], v_l[rows, :]), state)
        gv_all[rows, :] = gv[rows, :] + times_state_t((k_h[rows, :], k_l[rows, :]), state)
        for i, (src, dst) in enumerate(((gk_all, gk_hbm), (gv_all, gv_hbm))):
            store = pltpu.make_async_copy(src.at[rows, :], dst.at[rows, :], sem.at[2 * b + i])
            store.start()
            stores.append(store)
    for store in stores:
        store.wait()


def on_device(n_seq, n_head, query, key_in, value, out_grad, head_scale, norm_gain, group_counts):
    cap, d = query.shape
    block = 2 * GROUP if cap % (2 * GROUP) == 0 else GROUP
    half = -(-(cap // GROUP) // 8) * 8
    blocks = cap // block
    hbm = pl.BlockSpec(memory_space=pltpu.HBM)
    vmem = pl.BlockSpec(memory_space=pltpu.VMEM)
    wide = pltpu.VMEM((cap, d), F32)
    narrow = pltpu.VMEM((cap, d), BF16)
    state = pltpu.VMEM((d, d), F32)
    states = pltpu.VMEM((n_seq - 1, d, d), F32)
    rows = jax.ShapeDtypeStruct((cap, d), F32)
    rows_low = jax.ShapeDtypeStruct((cap, d), BF16)
    held = pl.pallas_call(
        functools.partial(kernel, n_seq, n_head, block),
        out_shape=[rows] * 4 + [rows_low] * 4 + [jax.ShapeDtypeStruct((d, d), F32)],
        in_specs=[pl.BlockSpec(memory_space=pltpu.SMEM)] + [hbm] * 6,
        out_specs=[vmem] * 9,
        scratch_shapes=[pltpu.SMEM(group_counts.shape, jnp.int32)]
        + [wide] * 4 + [pltpu.VMEM((d,), F32)]
        + [narrow] * 2 + [pltpu.VMEM((cap, block), BF16)] * 2
        + [pltpu.VMEM((d, cap), F32)] * 2 + [pltpu.VMEM((d, cap), BF16)] * 2
        + [state, states] * 2
        + [pltpu.VMEM((2 * half, GROUP), F32), pltpu.VMEM((n_head - 1, 2 * half, GROUP), F32)]
        + [pltpu.SemaphoreType.DMA((6,))]
        + [pltpu.SemaphoreType.DMA((n_seq - 1,))] * 4
        + [pltpu.SemaphoreType.DMA((n_head - 1,))] * 2,
        compiler_params=pltpu.CompilerParams(
            collective_id=0, has_side_effects=True, vmem_limit_bytes=32 * 1024 * 1024
        ),
    )(head_scale, *(
        pltpu.with_memory_space_constraint(x, pltpu.HBM)
        for x in (group_counts, query, key_in, value, out_grad, norm_gain)
    ))
    return pl.pallas_call(
        functools.partial(finish, block),
        out_shape=[rows] * 4,
        in_specs=[vmem] * 9,
        out_specs=[hbm] * 4,
        scratch_shapes=[wide] * 2 + [pltpu.SemaphoreType.DMA((2 * blocks + 2,))],
        compiler_params=pltpu.CompilerParams(vmem_limit_bytes=32 * 1024 * 1024),
    )(*held)


def solution(mesh):
    rows = P("seq", "head")
    return jax.shard_map(
        functools.partial(on_device, mesh.shape["seq"], mesh.shape["head"]),
        mesh=mesh,
        in_specs=(rows, rows, rows, rows, P("head"), P("head"), P()),
        out_specs=(rows, rows, rows, rows),
        check_vma=False,
    )
```

```python
import functools

import jax
import jax.numpy as jnp
from jax import lax
from jax.experimental import pallas as pl
from jax.experimental.pallas import tpu as pltpu
from jax.sharding import PartitionSpec as P

GROUP = 128
CHUNKS = 4
EPS = 1e-05
F32 = jnp.float32
BF16 = jnp.bfloat16
MESH = pl.DeviceIdType.MESH
NN = (((1,), (0,)), ((), ()))
NT = (((1,), (1,)), ((), ()))
TN = (((0,), (0,)), ((), ()))


def dot(left, right, dims):
    return lax.dot_general(left, right, dims, preferred_element_type=F32)


def split(x):
    high = x.astype(BF16)
    low = (x - high.astype(F32)).astype(BF16)
    return high, low


def beside(pair):
    return jnp.concatenate(pair, axis=1)


def add_rows(x):
    half = x.shape[0] // 2
    return x[:half] + x[half:]


def add_columns(x):
    half = x.shape[1] // 2
    return x[:, :half] + x[:, half:]


def stacked(s):
    top = jnp.concatenate([s[0], s[0]], axis=1)
    bottom = jnp.concatenate([s[1], jnp.zeros_like(s[1])], axis=1)
    return jnp.concatenate([top, bottom], axis=0)


def rows_by_rows(a, b):
    left = jnp.concatenate([a[0], a[1], a[0]], axis=1)
    right = jnp.concatenate([b[0], b[0], b[1]], axis=1)
    return dot(left, right, NT)


def rows_by_columns(a, b):
    left = jnp.concatenate([a[0], a[1], a[0]], axis=1)
    right = jnp.concatenate([b[0], b[0], b[1]], axis=0)
    return dot(left, right, NN)


def times(a, b):
    return add_columns(dot(a[0], beside(b), NN)) + dot(a[1], b[0], NN)


def columns_times(a, b):
    return add_columns(dot(a[0], beside(b), TN)) + dot(a[1], b[0], TN)


def times_state(a, s):
    top = jnp.concatenate([s[0], s[1]], axis=1)
    bottom = jnp.concatenate([s[0], jnp.zeros_like(s[0])], axis=1)
    return add_columns(dot(beside(a), jnp.concatenate([top, bottom], axis=0), NN))


def times_state_t(a, s):
    return add_columns(dot(beside(a), stacked(s), NT))


def state_by_rows(s, a):
    return add_rows(dot(s, beside(a), NT))


def outer(a, b):
    return add_rows(add_columns(dot(beside(a), beside(b), TN)))


def kernel(
    n_seq, n_head, block, head_scale, counts_hbm,
    q_hbm, k_hbm, v_hbm, g_hbm, gain_hbm,
    normed, gq, gk, gv, k_h, k_l, v_h, v_l, t_out,
    counts, q_in, k_in, v_in, g_in, gain,
    q_h, q_l, p_h, p_l, mine_t, gg_t, o_h, o_l,
    send_s, pass_s, near_s, far_s, send_t, pass_t, near_t, far_t, sums, sums_in,
    in_sem, h_send, h_recv, *seq_sems,
):
    cap, d = q_in.shape
    blocks = cap // block
    per = block // GROUP
    pos = lax.axis_index("seq")
    head = lax.axis_index("head")
    half = sums.shape[0] // 2

    s_sems, t_sems = seq_sems[:4], seq_sems[4:]

    barrier = pltpu.get_barrier_semaphore()
    for step in range(1, n_seq):
        pl.semaphore_signal(barrier, inc=1, device_id={"seq": lax.rem(pos + step, n_seq)}, device_id_type=MESH)
    loads = [
        pltpu.make_async_copy(src, dst, in_sem.at[i])
        for i, (src, dst) in enumerate(
            (
                (counts_hbm, counts), (k_hbm, k_in), (v_hbm, v_in), (q_hbm, q_in),
                (g_hbm, g_in), (gain_hbm, gain),
            )
        )
    ]
    for load in loads:
        load.start()
    for step in range(1, n_head):
        pl.semaphore_signal(barrier, inc=1, device_id={"head": lax.rem(head + step, n_head)}, device_id_type=MESH)

    def exchange(way, src, passed, near, far, sems):
        far_send, far_recv, near_send, near_recv = sems
        order = pos if way == 1 else n_seq - 1 - pos
        last = n_seq - 1
        direct = n_seq <= 4
        middle = jnp.logical_and(order > 0, order < (last - 1 if direct else last))
        heads_chain = jnp.logical_and(order == 0, last > (1 if direct else 0))

        def to_last():
            return pltpu.make_async_remote_copy(
                src_ref=src, dst_ref=far.at[order], send_sem=far_send, recv_sem=far_recv.at[order],
                device_id={"seq": last if way == 1 else 0}, device_id_type=MESH,
            )

        def from_order(k):
            return pltpu.make_async_remote_copy(
                src_ref=src, dst_ref=far.at[k], send_sem=far_send, recv_sem=far_recv.at[k],
                device_id={"seq": last if way == 1 else 0}, device_id_type=MESH,
            )

        def to_next(source, c):
            rows = pl.ds(c * (d // CHUNKS), d // CHUNKS)
            return pltpu.make_async_remote_copy(
                src_ref=source.at[rows, :], dst_ref=near.at[rows, :],
                send_sem=near_send.at[c], recv_sem=near_recv.at[c],
                device_id={"seq": pos + way}, device_id_type=MESH,
            )

        def clear():
            @pl.when(jnp.logical_or(order == 0, order == last) if direct else order == 0)
            def _():
                near[...] = jnp.zeros_like(near)

            if direct:

                @pl.when(order < last)
                def _():
                    far[...] = jnp.zeros_like(far)

        def start():
            if direct:

                @pl.when(order < last)
                def _():
                    to_last().start()

            @pl.when(heads_chain)
            def _():
                for c in range(CHUNKS):
                    to_next(src, c).start()

        def carried():
            @pl.when(middle)
            def _():
                for c in range(CHUNKS):
                    rows = pl.ds(c * (d // CHUNKS), d // CHUNKS)
                    to_next(src, c).wait_recv()
                    passed[rows, :] = src[rows, :] + near[rows, :]
                    to_next(passed, c).start()

            if direct:
                if last > 1:

                    @pl.when(order == last - 1)
                    def _():
                        for c in range(CHUNKS):
                            to_next(src, c).wait_recv()

                @pl.when(order == last)
                def _():
                    for k in range(last):
                        from_order(k).wait_recv()

            else:

                @pl.when(order == last)
                def _():
                    for c in range(CHUNKS):
                        to_next(src, c).wait_recv()

            total = near[...]
            if direct:
                for k in range(last):
                    total = total + far[k]
            return total

        def close():
            if direct:

                @pl.when(order < last)
                def _():
                    to_last().wait_send()

            @pl.when(jnp.logical_or(heads_chain, middle))
            def _():
                for c in range(CHUNKS):
                    to_next(src, c).wait_send()

        return clear, start, carried, close

    s_clear, s_start, s_carried, s_close = exchange(1, send_s, pass_s, near_s, far_s, s_sems)
    t_clear, t_start, t_carried, t_close = exchange(-1, send_t, pass_t, near_t, far_t, t_sems)
    s_clear()
    t_clear()

    row = lax.broadcasted_iota(jnp.int32, (block, d), 0)
    token = lax.broadcasted_iota(jnp.int32, (d, block), 1)
    upper = lax.broadcasted_iota(jnp.int32, (block, block), 0) <= lax.broadcasted_iota(jnp.int32, (block, block), 1)

    def take(b):
        return pl.ds(b * block, block)

    def pair(high, low, b):
        return high[take(b), :], low[take(b), :]

    loads[0].wait()
    live = counts[pos] * GROUP

    def keep(source, high, low, b):
        x = jnp.where(row + b * block < live, source[take(b), :], 0.0)
        high[take(b), :], low[take(b), :] = split(x)

    loads[1].wait()
    loads[2].wait()
    before = [jnp.zeros((d, d), F32)]
    for b in range(blocks):
        keep(k_in, k_h, k_l, b)
        keep(v_in, v_h, v_l, b)
        before.append(before[-1] + outer(pair(v_h, v_l, b), pair(k_h, k_l, b)))
    send_s[...] = before[-1]
    pl.semaphore_wait(barrier, n_head - 1 + n_seq - 1)
    s_start()

    loads[3].wait()
    loads[4].wait()
    loads[5].wait()
    scale = head_scale[0]
    gains = gain[...].reshape(1, d)
    for b in range(blocks):
        keep(q_in, q_h, q_l, b)
        q_b, k_b, v_b = pair(q_h, q_l, b), pair(k_h, k_l, b), pair(v_h, v_l, b)
        scores_t = split(jnp.where(upper, rows_by_rows(k_b, q_b), 0.0))
        p_h[take(b), :], p_l[take(b), :] = scores_t
        local = add_rows(dot(beside(v_b), scores_t[0], TN)) + dot(v_b[0], scores_t[1], TN)
        if b:
            local = local + state_by_rows(stacked(split(before[b])), q_b)
        mine_t[:, take(b)] = local
        gg_t[:, take(b)] = jnp.transpose(g_in[take(b), :] * gains)

    s_in = s_carried()
    arrived = stacked(split(s_in))
    for b in range(blocks):
        mine = (mine_t[:, take(b)] + state_by_rows(arrived, pair(q_h, q_l, b))) * scale
        mine_t[:, take(b)] = mine
        square = jnp.sum(mine * mine, axis=0, keepdims=True)
        cross = jnp.sum(gg_t[:, take(b)] * mine, axis=0, keepdims=True)
        for j in range(per):
            r = b * per + j
            sums[r : r + 1, :] = square[:, j * GROUP : (j + 1) * GROUP]
            sums[half + r : half + r + 1, :] = cross[:, j * GROUP : (j + 1) * GROUP]

    def partner(step):
        if n_head & (n_head - 1):
            return lax.rem(head + step, n_head)
        other, bit = head, 1
        while bit < n_head:
            if step & bit:
                other = other + bit - 2 * bit * lax.rem(head // bit, 2)
            bit *= 2
        return other

    shares = [
        pltpu.make_async_remote_copy(
            src_ref=sums, dst_ref=sums_in.at[step - 1],
            send_sem=h_send.at[step - 1], recv_sem=h_recv.at[step - 1],
            device_id={"head": partner(step)}, device_id_type=MESH,
        )
        for step in range(n_head - 1, 0, -1)
    ]
    for share in shares:
        share.start()
    total = sums[...]
    for share in shares:
        share.wait_recv()
    for step in range(1, n_head):
        total = total + sums_in[step - 1]
    features = d * n_head
    inverse = lax.rsqrt(total[:half] / features + EPS)
    factor = inverse * inverse * inverse * total[half:] / features

    def along(x, b):
        return jnp.concatenate([x[b * per + j : b * per + j + 1, :] for j in range(per)], axis=1)

    t_states = []
    for b in range(blocks):
        inv, fac = along(inverse, b), along(factor, b)
        grad = (gg_t[:, take(b)] * inv - mine_t[:, take(b)] * fac) * scale
        grad = split(jnp.where(token + b * block < live, grad, 0.0))
        o_h[:, take(b)], o_l[:, take(b)] = grad
        both = dot(jnp.concatenate(grad, axis=0), beside(pair(q_h, q_l, b)), NN)
        t_states.append(add_rows(add_columns(both)))
    after = [jnp.zeros((d, d), F32)]
    for b in range(blocks - 1, -1, -1):
        after.append(after[-1] + t_states[b])
    after = after[::-1]
    send_t[...] = after[0]
    t_start()

    for b in range(blocks):
        q_b, k_b, v_b = pair(q_h, q_l, b), pair(k_h, k_l, b), pair(v_h, v_l, b)
        o_t = o_h[:, take(b)], o_l[:, take(b)]
        o_b = jnp.transpose(o_t[0]), jnp.transpose(o_t[1])
        normed[take(b), :] = jnp.transpose(mine_t[:, take(b)] * along(inverse, b)) * gains
        pulled_t = split(jnp.where(upper, rows_by_columns(v_b, o_t), 0.0))
        gq[take(b), :] = times_state(o_b, split(s_in + before[b])) + columns_times(pulled_t, k_b)
        later = split(after[b + 1])
        gk[take(b), :] = times(pulled_t, q_b) + times_state(v_b, later)
        gv[take(b), :] = times(pair(p_h, p_l, b), o_b) + times_state_t(k_b, later)

    s_close()
    for share in shares:
        share.wait_send()
    t_out[...] = t_carried()
    t_close()


def finish(
    block, normed, gq, gk, gv, k_h, k_l, v_h, v_l, t_in,
    normed_hbm, gq_hbm, gk_hbm, gv_hbm, gk_all, gv_all, sem,
):
    blocks = gk.shape[0] // block
    stores = [
        pltpu.make_async_copy(normed, normed_hbm, sem.at[2 * blocks]),
        pltpu.make_async_copy(gq, gq_hbm, sem.at[2 * blocks + 1]),
    ]
    for store in stores:
        store.start()
    state = split(t_in[...])
    for b in range(blocks):
        rows = pl.ds(b * block, block)
        gk_all[rows, :] = gk[rows, :] + times_state((v_h[rows, :], v_l[rows, :]), state)
        gv_all[rows, :] = gv[rows, :] + times_state_t((k_h[rows, :], k_l[rows, :]), state)
        for i, (src, dst) in enumerate(((gk_all, gk_hbm), (gv_all, gv_hbm))):
            store = pltpu.make_async_copy(src.at[rows, :], dst.at[rows, :], sem.at[2 * b + i])
            store.start()
            stores.append(store)
    for store in stores:
        store.wait()


def on_device(n_seq, n_head, query, key_in, value, out_grad, head_scale, norm_gain, group_counts):
    cap, d = query.shape
    block = 2 * GROUP if cap % (2 * GROUP) == 0 else GROUP
    half = cap // GROUP
    blocks = cap // block
    hbm = pl.BlockSpec(memory_space=pltpu.HBM)
    vmem = pl.BlockSpec(memory_space=pltpu.VMEM)
    wide = pltpu.VMEM((cap, d), F32)
    narrow = pltpu.VMEM((cap, d), BF16)
    state = pltpu.VMEM((d, d), F32)
    states = pltpu.VMEM((n_seq - 1, d, d), F32)
    rows = jax.ShapeDtypeStruct((cap, d), F32)
    rows_low = jax.ShapeDtypeStruct((cap, d), BF16)
    held = pl.pallas_call(
        functools.partial(kernel, n_seq, n_head, block),
        out_shape=[rows] * 4 + [rows_low] * 4 + [jax.ShapeDtypeStruct((d, d), F32)],
        in_specs=[pl.BlockSpec(memory_space=pltpu.SMEM)] + [hbm] * 6,
        out_specs=[vmem] * 9,
        scratch_shapes=[pltpu.SMEM(group_counts.shape, jnp.int32)]
        + [wide] * 4 + [pltpu.VMEM((d,), F32)]
        + [narrow] * 2 + [pltpu.VMEM((cap, block), BF16)] * 2
        + [pltpu.VMEM((d, cap), F32)] * 2 + [pltpu.VMEM((d, cap), BF16)] * 2
        + [state, state, state, states] * 2
        + [pltpu.VMEM((2 * half, GROUP), F32), pltpu.VMEM((n_head - 1, 2 * half, GROUP), F32)]
        + [pltpu.SemaphoreType.DMA((6,))]
        + [pltpu.SemaphoreType.DMA((n_head - 1,))] * 2
        + [
            pltpu.SemaphoreType.DMA, pltpu.SemaphoreType.DMA((n_seq - 1,)),
            pltpu.SemaphoreType.DMA((CHUNKS,)), pltpu.SemaphoreType.DMA((CHUNKS,)),
        ] * 2,
        compiler_params=pltpu.CompilerParams(
            collective_id=0, has_side_effects=True, vmem_limit_bytes=32 * 1024 * 1024
        ),
    )(head_scale, *(
        pltpu.with_memory_space_constraint(x, pltpu.HBM)
        for x in (group_counts, query, key_in, value, out_grad, norm_gain)
    ))
    return pl.pallas_call(
        functools.partial(finish, block),
        out_shape=[rows] * 4,
        in_specs=[vmem] * 9,
        out_specs=[hbm] * 4,
        scratch_shapes=[wide] * 2 + [pltpu.SemaphoreType.DMA((2 * blocks + 2,))],
        compiler_params=pltpu.CompilerParams(vmem_limit_bytes=32 * 1024 * 1024),
    )(*held)


def solution(mesh):
    rows = P("seq", "head")
    return jax.shard_map(
        functools.partial(on_device, mesh.shape["seq"], mesh.shape["head"]),
        mesh=mesh,
        in_specs=(rows, rows, rows, rows, P("head"), P("head"), P()),
        out_specs=(rows, rows, rows, rows),
        check_vma=False,
    )
```

```python
import functools

import jax
import jax.numpy as jnp
from jax import lax
from jax.experimental import pallas as pl
from jax.experimental.pallas import tpu as pltpu
from jax.sharding import PartitionSpec as P

GROUP = 128
CHUNKS = 4
PARTS = 2
EPS = 1e-05
F32 = jnp.float32
BF16 = jnp.bfloat16
MESH = pl.DeviceIdType.MESH
NN = (((1,), (0,)), ((), ()))
NT = (((1,), (1,)), ((), ()))
TN = (((0,), (0,)), ((), ()))


def dot(left, right, dims):
    return lax.dot_general(left, right, dims, preferred_element_type=F32)


def split(x):
    high = x.astype(BF16)
    low = (x - high.astype(F32)).astype(BF16)
    return high, low


def beside(pair):
    return jnp.concatenate(pair, axis=1)


def add_rows(x):
    half = x.shape[0] // 2
    return x[:half] + x[half:]


def add_columns(x):
    half = x.shape[1] // 2
    return x[:, :half] + x[:, half:]


def stacked(s):
    top = jnp.concatenate([s[0], s[0]], axis=1)
    bottom = jnp.concatenate([s[1], jnp.zeros_like(s[1])], axis=1)
    return jnp.concatenate([top, bottom], axis=0)


def rows_by_rows(a, b):
    left = jnp.concatenate([a[0], a[1], a[0]], axis=1)
    right = jnp.concatenate([b[0], b[0], b[1]], axis=1)
    return dot(left, right, NT)


def rows_by_columns(a, b):
    left = jnp.concatenate([a[0], a[1], a[0]], axis=1)
    right = jnp.concatenate([b[0], b[0], b[1]], axis=0)
    return dot(left, right, NN)


def times(a, b):
    return add_columns(dot(a[0], beside(b), NN)) + dot(a[1], b[0], NN)


def columns_times(a, b):
    return add_columns(dot(a[0], beside(b), TN)) + dot(a[1], b[0], TN)


def times_state(a, s):
    top = jnp.concatenate([s[0], s[1]], axis=1)
    bottom = jnp.concatenate([s[0], jnp.zeros_like(s[0])], axis=1)
    return add_columns(dot(beside(a), jnp.concatenate([top, bottom], axis=0), NN))


def times_state_t(a, s):
    return add_columns(dot(beside(a), stacked(s), NT))


def state_by_rows(s, a):
    return add_rows(dot(s, beside(a), NT))


def outer(a, b):
    return add_rows(add_columns(dot(beside(a), beside(b), TN)))


def kernel(
    n_seq, n_head, block, head_scale, counts_hbm,
    q_hbm, k_hbm, v_hbm, g_hbm, gain_hbm,
    normed, gq, gk, gv, k_h, k_l, v_h, v_l, t_out,
    counts, q_in, k_in, v_in, g_in, gain,
    q_h, q_l, p_h, p_l, mine_t, gg_t, o_h, o_l,
    send_s, pass_s, near_s, far_s, send_t, pass_t, near_t, far_t, sums, sums_in,
    in_sem, h_send, h_recv, *seq_sems,
):
    cap, d = q_in.shape
    blocks = cap // block
    per = block // GROUP
    pos = lax.axis_index("seq")
    head = lax.axis_index("head")
    half = sums.shape[0] // 2

    s_sems, t_sems = seq_sems[:4], seq_sems[4:]

    barrier = pltpu.get_barrier_semaphore()
    for step in range(1, n_seq):
        pl.semaphore_signal(barrier, inc=1, device_id={"seq": lax.rem(pos + step, n_seq)}, device_id_type=MESH)
    loads = [
        pltpu.make_async_copy(src, dst, in_sem.at[i])
        for i, (src, dst) in enumerate(
            (
                (counts_hbm, counts), (k_hbm, k_in), (v_hbm, v_in), (q_hbm, q_in),
                (g_hbm, g_in), (gain_hbm, gain),
            )
        )
    ]
    for load in loads:
        load.start()
    for step in range(1, n_head):
        pl.semaphore_signal(barrier, inc=1, device_id={"head": lax.rem(head + step, n_head)}, device_id_type=MESH)

    def exchange(way, src, passed, near, far, sems):
        far_send, far_recv, near_send, near_recv = sems
        order = pos if way == 1 else n_seq - 1 - pos
        last = n_seq - 1
        direct = n_seq <= 4
        middle = jnp.logical_and(order > 0, order < (last - 1 if direct else last))
        heads_chain = jnp.logical_and(order == 0, last > (1 if direct else 0))

        def piece(p, parts):
            return pl.ds(p * (d // parts), d // parts)

        def far_copy(k, p):
            return pltpu.make_async_remote_copy(
                src_ref=src.at[piece(p, PARTS), :], dst_ref=far.at[k, piece(p, PARTS), :],
                send_sem=far_send.at[p], recv_sem=far_recv.at[k, p],
                device_id={"seq": last if way == 1 else 0}, device_id_type=MESH,
            )

        def to_next(source, c):
            rows = piece(c, CHUNKS)
            return pltpu.make_async_remote_copy(
                src_ref=source.at[rows, :], dst_ref=near.at[rows, :],
                send_sem=near_send.at[c], recv_sem=near_recv.at[c],
                device_id={"seq": pos + way}, device_id_type=MESH,
            )

        def clear():
            @pl.when(jnp.logical_or(order == 0, order == last) if direct else order == 0)
            def _():
                near[...] = jnp.zeros_like(near)

            if direct:

                @pl.when(order < last)
                def _():
                    far[...] = jnp.zeros_like(far)

        def start_last(p):
            if direct:

                @pl.when(order < last)
                def _():
                    far_copy(order, p).start()

        def start_next():
            @pl.when(heads_chain)
            def _():
                for c in range(CHUNKS):
                    to_next(src, c).start()

        def carried(p):
            per_part = CHUNKS // PARTS

            @pl.when(middle)
            def _():
                for c in range(p * per_part, (p + 1) * per_part):
                    rows = piece(c, CHUNKS)
                    to_next(src, c).wait_recv()
                    passed[rows, :] = src[rows, :] + near[rows, :]
                    to_next(passed, c).start()

            if not direct or last > 1:

                @pl.when(order == (last - 1 if direct else last))
                def _():
                    for c in range(p * per_part, (p + 1) * per_part):
                        to_next(src, c).wait_recv()

            if direct:

                @pl.when(order == last)
                def _():
                    for k in range(last):
                        far_copy(k, p).wait_recv()

            total = near[piece(p, PARTS), :]
            if direct:
                for k in range(last):
                    total = total + far[k, piece(p, PARTS), :]
            return total

        def close():
            if direct:

                @pl.when(order < last)
                def _():
                    for p in range(PARTS):
                        far_copy(order, p).wait_send()

            @pl.when(jnp.logical_or(heads_chain, middle))
            def _():
                for c in range(CHUNKS):
                    to_next(src, c).wait_send()

        return clear, start_last, start_next, carried, close

    s_clear, s_last, s_next, s_carried, s_close = exchange(1, send_s, pass_s, near_s, far_s, s_sems)
    t_clear, t_last, t_next, t_carried, t_close = exchange(-1, send_t, pass_t, near_t, far_t, t_sems)
    s_clear()
    t_clear()

    row = lax.broadcasted_iota(jnp.int32, (block, d), 0)
    upper = lax.broadcasted_iota(jnp.int32, (block, block), 0) <= lax.broadcasted_iota(jnp.int32, (block, block), 1)

    def take(b):
        return pl.ds(b * block, block)

    def pair(high, low, b):
        return high[take(b), :], low[take(b), :]

    loads[0].wait()
    live = counts[pos] * GROUP

    def keep(source, high, low, b):
        x = jnp.where(row + b * block < live, source[take(b), :], 0.0)
        high[take(b), :], low[take(b), :] = split(x)

    loads[1].wait()
    loads[2].wait()
    before = [jnp.zeros((d, d), F32)]
    for b in range(blocks):
        keep(k_in, k_h, k_l, b)
        keep(v_in, v_h, v_l, b)
        before.append(before[-1] + outer(pair(v_h, v_l, b), pair(k_h, k_l, b)))
    send_s[...] = before[-1]
    pl.semaphore_wait(barrier, n_head - 1 + n_seq - 1)
    s_next()
    for p in range(PARTS):
        s_last(p)

    loads[3].wait()
    loads[4].wait()
    loads[5].wait()
    scale = head_scale[0]
    gains = gain[...].reshape(1, d)
    for b in range(blocks):
        keep(q_in, q_h, q_l, b)
        q_b, k_b, v_b = pair(q_h, q_l, b), pair(k_h, k_l, b), pair(v_h, v_l, b)
        scores_t = split(jnp.where(upper, rows_by_rows(k_b, q_b), 0.0))
        p_h[take(b), :], p_l[take(b), :] = scores_t
        local = add_rows(dot(beside(v_b), scores_t[0], TN)) + dot(v_b[0], scores_t[1], TN)
        if b:
            local = local + state_by_rows(stacked(split(before[b])), q_b)
        mine_t[:, take(b)] = local
        gg_t[:, take(b)] = jnp.transpose(g_in[take(b), :] * gains)

    s_parts = []
    square, cross = [None] * blocks, [None] * blocks
    for p in range(PARTS):
        rows = pl.ds(p * (d // PARTS), d // PARTS)
        s_parts.append(s_carried(p))
        arrived = stacked(split(s_parts[p]))
        for b in range(blocks):
            mine = (mine_t[rows, take(b)] + state_by_rows(arrived, pair(q_h, q_l, b))) * scale
            mine_t[rows, take(b)] = mine
            squares = jnp.sum(mine * mine, axis=0, keepdims=True)
            crosses = jnp.sum(gg_t[rows, take(b)] * mine, axis=0, keepdims=True)
            square[b] = square[b] + squares if p else squares
            cross[b] = cross[b] + crosses if p else crosses
    s_in = jnp.concatenate(s_parts, axis=0)
    for b in range(blocks):
        for j in range(per):
            r = b * per + j
            sums[r : r + 1, :] = square[b][:, j * GROUP : (j + 1) * GROUP]
            sums[half + r : half + r + 1, :] = cross[b][:, j * GROUP : (j + 1) * GROUP]

    def partner(step):
        if n_head & (n_head - 1):
            return lax.rem(head + step, n_head)
        other, bit = head, 1
        while bit < n_head:
            if step & bit:
                other = other + bit - 2 * bit * lax.rem(head // bit, 2)
            bit *= 2
        return other

    shares = [
        pltpu.make_async_remote_copy(
            src_ref=sums, dst_ref=sums_in.at[step - 1],
            send_sem=h_send.at[step - 1], recv_sem=h_recv.at[step - 1],
            device_id={"head": partner(step)}, device_id_type=MESH,
        )
        for step in range(n_head - 1, 0, -1)
    ]
    for share in shares:
        share.start()
    total = sums[...]
    for share in shares:
        share.wait_recv()
    for step in range(1, n_head):
        total = total + sums_in[step - 1]
    features = d * n_head
    inverse = lax.rsqrt(total[:half] / features + EPS)
    factor = inverse * inverse * inverse * total[half:] / features

    def along(x, b):
        return jnp.concatenate([x[b * per + j : b * per + j + 1, :] for j in range(per)], axis=1)

    t_parts = [[] for _ in range(blocks)]
    for p in range(PARTS):
        rows = pl.ds(p * (d // PARTS), d // PARTS)
        token = lax.broadcasted_iota(jnp.int32, (d // PARTS, block), 1)
        whole = None
        for b in range(blocks):
            inv, fac = along(inverse, b), along(factor, b)
            grad = (gg_t[rows, take(b)] * inv - mine_t[rows, take(b)] * fac) * scale
            grad = split(jnp.where(token + b * block < live, grad, 0.0))
            o_h[rows, take(b)], o_l[rows, take(b)] = grad
            both = dot(jnp.concatenate(grad, axis=0), beside(pair(q_h, q_l, b)), NN)
            t_parts[b].append(add_rows(add_columns(both)))
            whole = t_parts[b][p] if whole is None else whole + t_parts[b][p]
        send_t[rows, :] = whole
        t_last(p)
    t_next()
    t_states = [jnp.concatenate(parts, axis=0) for parts in t_parts]
    after = [jnp.zeros((d, d), F32)]
    for b in range(blocks - 1, -1, -1):
        after.append(after[-1] + t_states[b])
    after = after[::-1]

    for b in range(blocks):
        q_b, k_b, v_b = pair(q_h, q_l, b), pair(k_h, k_l, b), pair(v_h, v_l, b)
        o_t = o_h[:, take(b)], o_l[:, take(b)]
        o_b = jnp.transpose(o_t[0]), jnp.transpose(o_t[1])
        normed[take(b), :] = jnp.transpose(mine_t[:, take(b)] * along(inverse, b)) * gains
        pulled_t = split(jnp.where(upper, rows_by_columns(v_b, o_t), 0.0))
        gq[take(b), :] = times_state(o_b, split(s_in + before[b])) + columns_times(pulled_t, k_b)
        later = split(after[b + 1])
        gk[take(b), :] = times(pulled_t, q_b) + times_state(v_b, later)
        gv[take(b), :] = times(pair(p_h, p_l, b), o_b) + times_state_t(k_b, later)

    s_close()
    for share in shares:
        share.wait_send()
    for p in range(PARTS):
        t_out[pl.ds(p * (d // PARTS), d // PARTS), :] = t_carried(p)
    t_close()


def finish(
    block, normed, gq, gk, gv, k_h, k_l, v_h, v_l, t_in,
    normed_hbm, gq_hbm, gk_hbm, gv_hbm, gk_all, gv_all, sem,
):
    blocks = gk.shape[0] // block
    stores = [
        pltpu.make_async_copy(normed, normed_hbm, sem.at[2 * blocks]),
        pltpu.make_async_copy(gq, gq_hbm, sem.at[2 * blocks + 1]),
    ]
    for store in stores:
        store.start()
    state = split(t_in[...])

    def save(src, dst, b, i):
        rows = pl.ds(b * block, block)
        store = pltpu.make_async_copy(src.at[rows, :], dst.at[rows, :], sem.at[2 * b + i])
        store.start()
        stores.append(store)

    for b in range(blocks):
        rows = pl.ds(b * block, block)
        gk_all[rows, :] = gk[rows, :] + times_state((v_h[rows, :], v_l[rows, :]), state)
        save(gk_all, gk_hbm, b, 0)
    for b in range(blocks):
        rows = pl.ds(b * block, block)
        gv_all[rows, :] = gv[rows, :] + times_state_t((k_h[rows, :], k_l[rows, :]), state)
        save(gv_all, gv_hbm, b, 1)
    for store in stores:
        store.wait()


def on_device(n_seq, n_head, query, key_in, value, out_grad, head_scale, norm_gain, group_counts):
    cap, d = query.shape
    block = 2 * GROUP if cap % (2 * GROUP) == 0 else GROUP
    half = cap // GROUP
    blocks = cap // block
    hbm = pl.BlockSpec(memory_space=pltpu.HBM)
    vmem = pl.BlockSpec(memory_space=pltpu.VMEM)
    wide = pltpu.VMEM((cap, d), F32)
    narrow = pltpu.VMEM((cap, d), BF16)
    state = pltpu.VMEM((d, d), F32)
    states = pltpu.VMEM((n_seq - 1, d, d), F32)
    rows = jax.ShapeDtypeStruct((cap, d), F32)
    rows_low = jax.ShapeDtypeStruct((cap, d), BF16)
    held = pl.pallas_call(
        functools.partial(kernel, n_seq, n_head, block),
        out_shape=[rows] * 4 + [rows_low] * 4 + [jax.ShapeDtypeStruct((d, d), F32)],
        in_specs=[pl.BlockSpec(memory_space=pltpu.SMEM)] + [hbm] * 6,
        out_specs=[vmem] * 9,
        scratch_shapes=[pltpu.SMEM(group_counts.shape, jnp.int32)]
        + [wide] * 4 + [pltpu.VMEM((d,), F32)]
        + [narrow] * 2 + [pltpu.VMEM((cap, block), BF16)] * 2
        + [pltpu.VMEM((d, cap), F32)] * 2 + [pltpu.VMEM((d, cap), BF16)] * 2
        + [state, state, state, states] * 2
        + [pltpu.VMEM((2 * half, GROUP), F32), pltpu.VMEM((n_head - 1, 2 * half, GROUP), F32)]
        + [pltpu.SemaphoreType.DMA((6,))]
        + [pltpu.SemaphoreType.DMA((n_head - 1,))] * 2
        + [
            pltpu.SemaphoreType.DMA((PARTS,)), pltpu.SemaphoreType.DMA((n_seq - 1, PARTS)),
            pltpu.SemaphoreType.DMA((CHUNKS,)), pltpu.SemaphoreType.DMA((CHUNKS,)),
        ] * 2,
        compiler_params=pltpu.CompilerParams(
            collective_id=0, has_side_effects=True, vmem_limit_bytes=32 * 1024 * 1024
        ),
    )(head_scale, *(
        pltpu.with_memory_space_constraint(x, pltpu.HBM)
        for x in (group_counts, query, key_in, value, out_grad, norm_gain)
    ))
    return pl.pallas_call(
        functools.partial(finish, block),
        out_shape=[rows] * 4,
        in_specs=[vmem] * 9,
        out_specs=[hbm] * 4,
        scratch_shapes=[wide] * 2 + [pltpu.SemaphoreType.DMA((2 * blocks + 2,))],
        compiler_params=pltpu.CompilerParams(vmem_limit_bytes=32 * 1024 * 1024),
    )(*held)


def solution(mesh):
    rows = P("seq", "head")
    return jax.shard_map(
        functools.partial(on_device, mesh.shape["seq"], mesh.shape["head"]),
        mesh=mesh,
        in_specs=(rows, rows, rows, rows, P("head"), P("head"), P()),
        out_specs=(rows, rows, rows, rows),
        check_vma=False,
    )
```

```python
import functools

import jax
import jax.numpy as jnp
from jax import lax
from jax.experimental import pallas as pl
from jax.experimental.pallas import tpu as pltpu
from jax.sharding import PartitionSpec as P

GROUP = 128
CHUNKS = 4
PARTS = 2
EPS = 1e-05
F32 = jnp.float32
BF16 = jnp.bfloat16
MESH = pl.DeviceIdType.MESH
NN = (((1,), (0,)), ((), ()))
NT = (((1,), (1,)), ((), ()))
TN = (((0,), (0,)), ((), ()))


def dot(left, right, dims):
    return lax.dot_general(left, right, dims, preferred_element_type=F32)


def split(x):
    high = x.astype(BF16)
    low = (x - high.astype(F32)).astype(BF16)
    return high, low


def beside(pair):
    return jnp.concatenate(pair, axis=1)


def add_rows(x):
    half = x.shape[0] // 2
    return x[:half] + x[half:]


def add_columns(x):
    half = x.shape[1] // 2
    return x[:, :half] + x[:, half:]


def stacked(s):
    top = jnp.concatenate([s[0], s[0]], axis=1)
    bottom = jnp.concatenate([s[1], jnp.zeros_like(s[1])], axis=1)
    return jnp.concatenate([top, bottom], axis=0)


def rows_by_rows(a, b):
    left = jnp.concatenate([a[0], a[1], a[0]], axis=1)
    right = jnp.concatenate([b[0], b[0], b[1]], axis=1)
    return dot(left, right, NT)


def rows_by_columns(a, b):
    left = jnp.concatenate([a[0], a[1], a[0]], axis=1)
    right = jnp.concatenate([b[0], b[0], b[1]], axis=0)
    return dot(left, right, NN)


def times(a, b):
    return add_columns(dot(a[0], beside(b), NN)) + dot(a[1], b[0], NN)


def columns_times(a, b):
    return add_columns(dot(a[0], beside(b), TN)) + dot(a[1], b[0], TN)


def times_state(a, s):
    top = jnp.concatenate([s[0], s[1]], axis=1)
    bottom = jnp.concatenate([s[0], jnp.zeros_like(s[0])], axis=1)
    return add_columns(dot(beside(a), jnp.concatenate([top, bottom], axis=0), NN))


def times_state_t(a, s):
    return add_columns(dot(beside(a), stacked(s), NT))


def state_by_rows(s, a):
    return add_rows(dot(s, beside(a), NT))


def outer(a, b):
    return add_rows(add_columns(dot(beside(a), beside(b), TN)))


def kernel(
    n_seq, n_head, block, head_scale, counts_hbm,
    q_hbm, k_hbm, v_hbm, g_hbm, gain_hbm,
    normed, gq, gk, gv, k_h, k_l, v_h, v_l, t_out,
    counts, q_in, k_in, v_in, g_in, gain,
    q_h, q_l, p_h, p_l, mine_t, gg_t, o_h, o_l,
    send_s, pass_s, near_s, far_s, send_t, pass_t, near_t, far_t, sums, sums_in,
    in_sem, h_send, h_recv, *seq_sems,
):
    cap, d = q_in.shape
    blocks = cap // block
    per = block // GROUP
    pos = lax.axis_index("seq")
    head = lax.axis_index("head")
    half = sums.shape[0] // 2
    second = lax.rem(head, 2) == 1

    s_sems, t_sems = seq_sems[:4], seq_sems[4:]

    barrier = pltpu.get_barrier_semaphore()
    for step in range(1, n_seq):
        pl.semaphore_signal(barrier, inc=1, device_id={"seq": lax.rem(pos + step, n_seq)}, device_id_type=MESH)
    loads = [
        pltpu.make_async_copy(src, dst, in_sem.at[i])
        for i, (src, dst) in enumerate(
            (
                (counts_hbm, counts), (k_hbm, k_in), (v_hbm, v_in), (q_hbm, q_in),
                (g_hbm, g_in), (gain_hbm, gain),
            )
        )
    ]
    for load in loads:
        load.start()
    for step in range(1, n_head):
        pl.semaphore_signal(barrier, inc=1, device_id={"head": lax.rem(head + step, n_head)}, device_id_type=MESH)

    def exchange(way, src, passed, near, far, sems):
        far_send, far_recv, near_send, near_recv = sems
        order = pos if way == 1 else n_seq - 1 - pos
        last = n_seq - 1
        direct = n_seq <= 4
        middle = jnp.logical_and(order > 0, order < (last - 1 if direct else last))
        heads_chain = jnp.logical_and(order == 0, last > (1 if direct else 0))

        merge = way == -1 and direct and last == 3
        merged = jnp.logical_and(second, order <= 1) if merge else False

        def piece(p, parts):
            return pl.ds(p * (d // parts), d // parts)

        def far_copy(k, p, source=src):
            return pltpu.make_async_remote_copy(
                src_ref=source.at[piece(p, PARTS), :], dst_ref=far.at[k, piece(p, PARTS), :],
                send_sem=far_send.at[p], recv_sem=far_recv.at[k, p],
                device_id={"seq": last if way == 1 else 0}, device_id_type=MESH,
            )

        def to_next(source, c):
            rows = piece(c, CHUNKS)
            return pltpu.make_async_remote_copy(
                src_ref=source.at[rows, :], dst_ref=near.at[rows, :],
                send_sem=near_send.at[c], recv_sem=near_recv.at[c],
                device_id={"seq": pos + way}, device_id_type=MESH,
            )

        def clear():
            @pl.when(jnp.logical_or(order == 0, order == last) if direct else order == 0)
            def _():
                near[...] = jnp.zeros_like(near)

            if direct:

                @pl.when(order < last)
                def _():
                    far[...] = jnp.zeros_like(far)

                if merge:

                    @pl.when(jnp.logical_and(order == last, second))
                    def _():
                        far[0] = jnp.zeros(far.shape[1:], F32)

        def start_last(p):
            if direct:

                @pl.when(jnp.logical_and(order < last, jnp.logical_not(merged)))
                def _():
                    far_copy(order, p).start()

        def start_next():
            @pl.when(heads_chain)
            def _():
                for c in range(CHUNKS):
                    to_next(src, c).start()

        def relay(p, when):
            chunks = range(p * (CHUNKS // PARTS), (p + 1) * (CHUNKS // PARTS))

            def pass_on():
                for c in chunks:
                    to_next(passed, c).start()

            @pl.when(jnp.logical_and(middle, when))
            def _():
                for c in chunks:
                    rows = piece(c, CHUNKS)
                    to_next(src, c).wait_recv()
                    passed[rows, :] = src[rows, :] + near[rows, :]
                    if not merge:
                        to_next(passed, c).start()

                if merge:

                    @pl.when(merged)
                    def _():
                        far_copy(1, p, passed).start()

                        if p == PARTS - 1:
                            for c in range(CHUNKS):
                                to_next(passed, c).start()

                    @pl.when(jnp.logical_not(merged))
                    def _():
                        pass_on()

        def carried(p):
            per_part = CHUNKS // PARTS

            if not direct or last > 1:

                @pl.when(order == (last - 1 if direct else last))
                def _():
                    for c in range(p * per_part, (p + 1) * per_part):
                        to_next(src, c).wait_recv()

            if direct:

                @pl.when(order == last)
                def _():
                    for k in range(1 if merge else 0, last):
                        far_copy(k, p).wait_recv()

                if merge:

                    @pl.when(jnp.logical_and(order == last, jnp.logical_not(second)))
                    def _():
                        far_copy(0, p).wait_recv()

            total = near[piece(p, PARTS), :]
            if direct:
                for k in range(last):
                    total = total + far[k, piece(p, PARTS), :]
            return total

        def close():
            if direct:

                @pl.when(jnp.logical_and(order < last, jnp.logical_or(order > 0, jnp.logical_not(merged))))
                def _():
                    for p in range(PARTS):
                        far_copy(order, p).wait_send()

            @pl.when(jnp.logical_or(heads_chain, middle))
            def _():
                for c in range(CHUNKS):
                    to_next(src, c).wait_send()

        return clear, start_last, start_next, relay, carried, close

    s_clear, s_last, s_next, s_relay, s_carried, s_close = exchange(1, send_s, pass_s, near_s, far_s, s_sems)
    t_clear, t_last, t_next, t_relay, t_carried, t_close = exchange(-1, send_t, pass_t, near_t, far_t, t_sems)
    s_clear()
    t_clear()

    row = lax.broadcasted_iota(jnp.int32, (block, d), 0)
    upper = lax.broadcasted_iota(jnp.int32, (block, block), 0) <= lax.broadcasted_iota(jnp.int32, (block, block), 1)

    def take(b):
        return pl.ds(b * block, block)

    def pair(high, low, b):
        return high[take(b), :], low[take(b), :]

    loads[0].wait()
    live = counts[pos] * GROUP

    def keep(source, high, low, b):
        x = jnp.where(row + b * block < live, source[take(b), :], 0.0)
        high[take(b), :], low[take(b), :] = split(x)

    loads[1].wait()
    loads[2].wait()
    before = [jnp.zeros((d, d), F32)]
    for b in range(blocks):
        keep(k_in, k_h, k_l, b)
        keep(v_in, v_h, v_l, b)
        before.append(before[-1] + outer(pair(v_h, v_l, b), pair(k_h, k_l, b)))
    send_s[...] = before[-1]
    pl.semaphore_wait(barrier, n_head - 1 + n_seq - 1)
    s_next()
    for p in range(PARTS):
        s_last(p)

    loads[3].wait()
    loads[4].wait()
    loads[5].wait()
    scale = head_scale[0]
    gains = gain[...].reshape(1, d)
    for b in range(blocks):
        keep(q_in, q_h, q_l, b)
        q_b, k_b, v_b = pair(q_h, q_l, b), pair(k_h, k_l, b), pair(v_h, v_l, b)
        scores_t = split(jnp.where(upper, rows_by_rows(k_b, q_b), 0.0))
        p_h[take(b), :], p_l[take(b), :] = scores_t
        local = add_rows(dot(beside(v_b), scores_t[0], TN)) + dot(v_b[0], scores_t[1], TN)
        if b:
            local = local + state_by_rows(stacked(split(before[b])), q_b)
        mine_t[:, take(b)] = local
        gg_t[:, take(b)] = jnp.transpose(g_in[take(b), :] * gains)

    s_parts = []
    square, cross = [None] * blocks, [None] * blocks
    for p in range(PARTS):
        rows = pl.ds(p * (d // PARTS), d // PARTS)
        s_relay(p, True)
        s_parts.append(s_carried(p))
        arrived = stacked(split(s_parts[p]))
        for b in range(blocks):
            mine = (mine_t[rows, take(b)] + state_by_rows(arrived, pair(q_h, q_l, b))) * scale
            mine_t[rows, take(b)] = mine
            squares = jnp.sum(mine * mine, axis=0, keepdims=True)
            crosses = jnp.sum(gg_t[rows, take(b)] * mine, axis=0, keepdims=True)
            square[b] = square[b] + squares if p else squares
            cross[b] = cross[b] + crosses if p else crosses
    s_in = jnp.concatenate(s_parts, axis=0)
    for b in range(blocks):
        for j in range(per):
            r = b * per + j
            sums[r : r + 1, :] = square[b][:, j * GROUP : (j + 1) * GROUP]
            sums[half + r : half + r + 1, :] = cross[b][:, j * GROUP : (j + 1) * GROUP]

    def partner(step):
        if n_head & (n_head - 1):
            return lax.rem(head + step, n_head)
        other, bit = head, 1
        while bit < n_head:
            if step & bit:
                other = other + bit - 2 * bit * lax.rem(head // bit, 2)
            bit *= 2
        return other

    shares = [
        pltpu.make_async_remote_copy(
            src_ref=sums, dst_ref=sums_in.at[step - 1],
            send_sem=h_send.at[step - 1], recv_sem=h_recv.at[step - 1],
            device_id={"head": partner(step)}, device_id_type=MESH,
        )
        for step in range(n_head - 1, 0, -1)
    ]
    for share in shares:
        share.start()
    total = sums[...]
    for share in shares:
        share.wait_recv()
    for step in range(1, n_head):
        total = total + sums_in[step - 1]
    features = d * n_head
    inverse = lax.rsqrt(total[:half] / features + EPS)
    factor = inverse * inverse * inverse * total[half:] / features

    def along(x, b):
        return jnp.concatenate([x[b * per + j : b * per + j + 1, :] for j in range(per)], axis=1)

    t_parts = [[] for _ in range(blocks)]
    for p in range(PARTS):
        rows = pl.ds(p * (d // PARTS), d // PARTS)
        token = lax.broadcasted_iota(jnp.int32, (d // PARTS, block), 1)
        whole = None
        for b in range(blocks):
            inv, fac = along(inverse, b), along(factor, b)
            grad = (gg_t[rows, take(b)] * inv - mine_t[rows, take(b)] * fac) * scale
            grad = split(jnp.where(token + b * block < live, grad, 0.0))
            o_h[rows, take(b)], o_l[rows, take(b)] = grad
            both = dot(jnp.concatenate(grad, axis=0), beside(pair(q_h, q_l, b)), NN)
            t_parts[b].append(add_rows(add_columns(both)))
            whole = t_parts[b][p] if whole is None else whole + t_parts[b][p]
        send_t[rows, :] = whole
        t_last(p)
    t_next()
    t_states = [jnp.concatenate(parts, axis=0) for parts in t_parts]
    after = [jnp.zeros((d, d), F32)]
    for b in range(blocks - 1, -1, -1):
        after.append(after[-1] + t_states[b])
    after = after[::-1]

    for b in range(blocks):
        q_b, k_b, v_b = pair(q_h, q_l, b), pair(k_h, k_l, b), pair(v_h, v_l, b)
        o_t = o_h[:, take(b)], o_l[:, take(b)]
        o_b = jnp.transpose(o_t[0]), jnp.transpose(o_t[1])
        normed[take(b), :] = jnp.transpose(mine_t[:, take(b)] * along(inverse, b)) * gains
        pulled_t = split(jnp.where(upper, rows_by_columns(v_b, o_t), 0.0))
        gq[take(b), :] = times_state(o_b, split(s_in + before[b])) + columns_times(pulled_t, k_b)
        later = split(after[b + 1])
        gk[take(b), :] = times(pulled_t, q_b) + times_state(v_b, later)
        gv[take(b), :] = times(pair(p_h, p_l, b), o_b) + times_state_t(k_b, later)
        if b == 1:
            for p in range(PARTS):
                t_relay(p, second)

    s_close()
    for share in shares:
        share.wait_send()
    for p in range(PARTS):
        t_relay(p, jnp.logical_not(second))
        t_out[pl.ds(p * (d // PARTS), d // PARTS), :] = t_carried(p)
    t_close()


def finish(
    block, normed, gq, gk, gv, k_h, k_l, v_h, v_l, t_in,
    normed_hbm, gq_hbm, gk_hbm, gv_hbm, gk_all, gv_all, sem,
):
    blocks = gk.shape[0] // block
    stores = [
        pltpu.make_async_copy(normed, normed_hbm, sem.at[2 * blocks]),
        pltpu.make_async_copy(gq, gq_hbm, sem.at[2 * blocks + 1]),
    ]
    for store in stores:
        store.start()
    state = split(t_in[...])

    def save(src, dst, b, i):
        rows = pl.ds(b * block, block)
        store = pltpu.make_async_copy(src.at[rows, :], dst.at[rows, :], sem.at[2 * b + i])
        store.start()
        stores.append(store)

    for b in range(blocks):
        rows = pl.ds(b * block, block)
        gk_all[rows, :] = gk[rows, :] + times_state((v_h[rows, :], v_l[rows, :]), state)
        save(gk_all, gk_hbm, b, 0)
    for b in range(blocks):
        rows = pl.ds(b * block, block)
        gv_all[rows, :] = gv[rows, :] + times_state_t((k_h[rows, :], k_l[rows, :]), state)
        save(gv_all, gv_hbm, b, 1)
    for store in stores:
        store.wait()


def on_device(n_seq, n_head, query, key_in, value, out_grad, head_scale, norm_gain, group_counts):
    cap, d = query.shape
    block = 2 * GROUP if cap % (2 * GROUP) == 0 else GROUP
    half = cap // GROUP
    blocks = cap // block
    hbm = pl.BlockSpec(memory_space=pltpu.HBM)
    vmem = pl.BlockSpec(memory_space=pltpu.VMEM)
    wide = pltpu.VMEM((cap, d), F32)
    narrow = pltpu.VMEM((cap, d), BF16)
    state = pltpu.VMEM((d, d), F32)
    states = pltpu.VMEM((n_seq - 1, d, d), F32)
    rows = jax.ShapeDtypeStruct((cap, d), F32)
    rows_low = jax.ShapeDtypeStruct((cap, d), BF16)
    held = pl.pallas_call(
        functools.partial(kernel, n_seq, n_head, block),
        out_shape=[rows] * 4 + [rows_low] * 4 + [jax.ShapeDtypeStruct((d, d), F32)],
        in_specs=[pl.BlockSpec(memory_space=pltpu.SMEM)] + [hbm] * 6,
        out_specs=[vmem] * 9,
        scratch_shapes=[pltpu.SMEM(group_counts.shape, jnp.int32)]
        + [wide] * 4 + [pltpu.VMEM((d,), F32)]
        + [narrow] * 2 + [pltpu.VMEM((cap, block), BF16)] * 2
        + [pltpu.VMEM((d, cap), F32)] * 2 + [pltpu.VMEM((d, cap), BF16)] * 2
        + [state, state, state, states] * 2
        + [pltpu.VMEM((2 * half, GROUP), F32), pltpu.VMEM((n_head - 1, 2 * half, GROUP), F32)]
        + [pltpu.SemaphoreType.DMA((6,))]
        + [pltpu.SemaphoreType.DMA((n_head - 1,))] * 2
        + [
            pltpu.SemaphoreType.DMA((PARTS,)), pltpu.SemaphoreType.DMA((n_seq - 1, PARTS)),
            pltpu.SemaphoreType.DMA((CHUNKS,)), pltpu.SemaphoreType.DMA((CHUNKS,)),
        ] * 2,
        compiler_params=pltpu.CompilerParams(
            collective_id=0, has_side_effects=True, vmem_limit_bytes=32 * 1024 * 1024
        ),
    )(head_scale, *(
        pltpu.with_memory_space_constraint(x, pltpu.HBM)
        for x in (group_counts, query, key_in, value, out_grad, norm_gain)
    ))
    return pl.pallas_call(
        functools.partial(finish, block),
        out_shape=[rows] * 4,
        in_specs=[vmem] * 9,
        out_specs=[hbm] * 4,
        scratch_shapes=[wide] * 2 + [pltpu.SemaphoreType.DMA((2 * blocks + 2,))],
        compiler_params=pltpu.CompilerParams(vmem_limit_bytes=32 * 1024 * 1024),
    )(*held)


def solution(mesh):
    rows = P("seq", "head")
    return jax.shard_map(
        functools.partial(on_device, mesh.shape["seq"], mesh.shape["head"]),
        mesh=mesh,
        in_specs=(rows, rows, rows, rows, P("head"), P("head"), P()),
        out_specs=(rows, rows, rows, rows),
        check_vma=False,
    )
```

```python
import functools

import jax
import jax.numpy as jnp
from jax import lax
from jax.experimental import pallas as pl
from jax.experimental.pallas import tpu as pltpu
from jax.sharding import PartitionSpec as P

GROUP = 128
CHUNKS = 2
PARTS = 2
EPS = 1e-05
F32 = jnp.float32
BF16 = jnp.bfloat16
MESH = pl.DeviceIdType.MESH
NN = (((1,), (0,)), ((), ()))
NT = (((1,), (1,)), ((), ()))
TN = (((0,), (0,)), ((), ()))


def dot(left, right, dims):
    return lax.dot_general(left, right, dims, preferred_element_type=F32)


def split(x):
    high = x.astype(BF16)
    low = (x - high.astype(F32)).astype(BF16)
    return high, low


def beside(pair):
    return jnp.concatenate(pair, axis=1)


def add_rows(x):
    half = x.shape[0] // 2
    return x[:half] + x[half:]


def add_columns(x):
    half = x.shape[1] // 2
    return x[:, :half] + x[:, half:]


def stacked(s):
    top = jnp.concatenate([s[0], s[0]], axis=1)
    bottom = jnp.concatenate([s[1], jnp.zeros_like(s[1])], axis=1)
    return jnp.concatenate([top, bottom], axis=0)


def rows_by_rows(a, b):
    left = jnp.concatenate([a[0], a[1], a[0]], axis=1)
    right = jnp.concatenate([b[0], b[0], b[1]], axis=1)
    return dot(left, right, NT)


def rows_by_columns(a, b):
    left = jnp.concatenate([a[0], a[1], a[0]], axis=1)
    right = jnp.concatenate([b[0], b[0], b[1]], axis=0)
    return dot(left, right, NN)


def times(a, b):
    return add_columns(dot(a[0], beside(b), NN)) + dot(a[1], b[0], NN)


def columns_times(a, b):
    return add_columns(dot(a[0], beside(b), TN)) + dot(a[1], b[0], TN)


def times_state(a, s):
    top = jnp.concatenate([s[0], s[1]], axis=1)
    bottom = jnp.concatenate([s[0], jnp.zeros_like(s[0])], axis=1)
    return add_columns(dot(beside(a), jnp.concatenate([top, bottom], axis=0), NN))


def times_state_t(a, s):
    return add_columns(dot(beside(a), stacked(s), NT))


def state_by_rows(s, a):
    return add_rows(dot(s, beside(a), NT))


def outer(a, b):
    return add_rows(add_columns(dot(beside(a), beside(b), TN)))


def kernel(
    n_seq, n_head, block, head_scale, counts_hbm,
    q_hbm, k_hbm, v_hbm, g_hbm, gain_hbm,
    normed, gq, gk, gv, k_h, k_l, v_h, v_l, t_out,
    counts, q_in, k_in, v_in, g_in, gain,
    q_h, q_l, p_h, p_l, mine_t, gg_t, o_h, o_l,
    send_s, pass_s, near_s, far_s, send_t, pass_t, near_t, far_t, sums, sums_in,
    in_sem, h_send, h_recv, *seq_sems,
):
    cap, d = q_in.shape
    blocks = cap // block
    per = block // GROUP
    pos = lax.axis_index("seq")
    head = lax.axis_index("head")
    half = sums.shape[0] // 2
    second = lax.rem(head, 2) == 1

    s_sems, t_sems = seq_sems[:4], seq_sems[4:]

    barrier = pltpu.get_barrier_semaphore()
    for step in range(1, n_seq):
        pl.semaphore_signal(barrier, inc=1, device_id={"seq": lax.rem(pos + step, n_seq)}, device_id_type=MESH)
    loads = [
        pltpu.make_async_copy(src, dst, in_sem.at[i])
        for i, (src, dst) in enumerate(
            (
                (counts_hbm, counts), (k_hbm, k_in), (v_hbm, v_in), (q_hbm, q_in),
                (g_hbm, g_in), (gain_hbm, gain),
            )
        )
    ]
    for load in loads:
        load.start()
    for step in range(1, n_head):
        pl.semaphore_signal(barrier, inc=1, device_id={"head": lax.rem(head + step, n_head)}, device_id_type=MESH)

    def exchange(way, src, passed, near, far, sems):
        far_send, far_recv, near_send, near_recv = sems
        order = pos if way == 1 else n_seq - 1 - pos
        last = n_seq - 1
        direct = n_seq <= 4
        middle = jnp.logical_and(order > 0, order < (last - 1 if direct else last))
        heads_chain = jnp.logical_and(order == 0, last > (1 if direct else 0))

        merge = direct and last == 3
        merged = jnp.logical_and(second, order <= 1) if merge else False

        def piece(p, parts):
            return pl.ds(p * (d // parts), d // parts)

        def far_copy(k, p, source=src):
            return pltpu.make_async_remote_copy(
                src_ref=source.at[piece(p, PARTS), :], dst_ref=far.at[k, piece(p, PARTS), :],
                send_sem=far_send.at[p], recv_sem=far_recv.at[k, p],
                device_id={"seq": last if way == 1 else 0}, device_id_type=MESH,
            )

        def to_next(source, c):
            rows = piece(c, CHUNKS)
            return pltpu.make_async_remote_copy(
                src_ref=source.at[rows, :], dst_ref=near.at[rows, :],
                send_sem=near_send.at[c], recv_sem=near_recv.at[c],
                device_id={"seq": pos + way}, device_id_type=MESH,
            )

        def clear():
            @pl.when(jnp.logical_or(order == 0, order == last) if direct else order == 0)
            def _():
                near[...] = jnp.zeros_like(near)

            if direct:

                @pl.when(order < last)
                def _():
                    far[...] = jnp.zeros_like(far)

                if merge:

                    @pl.when(jnp.logical_and(order == last, second))
                    def _():
                        far[0] = jnp.zeros(far.shape[1:], F32)

        def start_last(p):
            if direct:

                @pl.when(jnp.logical_and(order < last, jnp.logical_not(merged)))
                def _():
                    far_copy(order, p).start()

        def start_next():
            @pl.when(heads_chain)
            def _():
                for c in range(CHUNKS):
                    to_next(src, c).start()

        def relay(p, when):
            chunks = range(p * (CHUNKS // PARTS), (p + 1) * (CHUNKS // PARTS))

            def pass_on():
                for c in chunks:
                    to_next(passed, c).start()

            @pl.when(jnp.logical_and(middle, when))
            def _():
                for c in chunks:
                    rows = piece(c, CHUNKS)
                    to_next(src, c).wait_recv()
                    passed[rows, :] = src[rows, :] + near[rows, :]
                    if not merge:
                        to_next(passed, c).start()

                if merge:

                    @pl.when(merged)
                    def _():
                        far_copy(1, p, passed).start()

                        if p == PARTS - 1:
                            for c in range(CHUNKS):
                                to_next(passed, c).start()

                    @pl.when(jnp.logical_not(merged))
                    def _():
                        pass_on()

        def carried(p):
            per_part = CHUNKS // PARTS

            if not direct or last > 1:

                @pl.when(order == (last - 1 if direct else last))
                def _():
                    for c in range(p * per_part, (p + 1) * per_part):
                        to_next(src, c).wait_recv()

            if direct:

                @pl.when(order == last)
                def _():
                    for k in range(1 if merge else 0, last):
                        far_copy(k, p).wait_recv()

                if merge:

                    @pl.when(jnp.logical_and(order == last, jnp.logical_not(second)))
                    def _():
                        far_copy(0, p).wait_recv()

            total = near[piece(p, PARTS), :]
            if direct:
                for k in range(last):
                    total = total + far[k, piece(p, PARTS), :]
            return total

        def close():
            if direct:

                @pl.when(jnp.logical_and(order < last, jnp.logical_or(order > 0, jnp.logical_not(merged))))
                def _():
                    for p in range(PARTS):
                        far_copy(order, p).wait_send()

            @pl.when(jnp.logical_or(heads_chain, middle))
            def _():
                for c in range(CHUNKS):
                    to_next(src, c).wait_send()

        return clear, start_last, start_next, relay, carried, close

    s_clear, s_last, s_next, s_relay, s_carried, s_close = exchange(1, send_s, pass_s, near_s, far_s, s_sems)
    t_clear, t_last, t_next, t_relay, t_carried, t_close = exchange(-1, send_t, pass_t, near_t, far_t, t_sems)
    s_clear()
    t_clear()

    row = lax.broadcasted_iota(jnp.int32, (block, d), 0)
    upper = lax.broadcasted_iota(jnp.int32, (block, block), 0) <= lax.broadcasted_iota(jnp.int32, (block, block), 1)

    def take(b):
        return pl.ds(b * block, block)

    def pair(high, low, b):
        return high[take(b), :], low[take(b), :]

    loads[0].wait()
    live = counts[pos] * GROUP

    def keep(source, high, low, b):
        x = jnp.where(row + b * block < live, source[take(b), :], 0.0)
        high[take(b), :], low[take(b), :] = split(x)

    loads[1].wait()
    loads[2].wait()
    before = [jnp.zeros((d, d), F32)]
    for b in range(blocks):
        keep(k_in, k_h, k_l, b)
        keep(v_in, v_h, v_l, b)
        before.append(before[-1] + outer(pair(v_h, v_l, b), pair(k_h, k_l, b)))
    send_s[...] = before[-1]
    pl.semaphore_wait(barrier, n_head - 1 + n_seq - 1)
    s_next()
    for p in range(PARTS):
        s_last(p)

    loads[3].wait()
    loads[4].wait()
    loads[5].wait()
    scale = head_scale[0]
    gains = gain[...].reshape(1, d)
    for b in range(blocks):
        keep(q_in, q_h, q_l, b)
        q_b, k_b, v_b = pair(q_h, q_l, b), pair(k_h, k_l, b), pair(v_h, v_l, b)
        scores_t = split(jnp.where(upper, rows_by_rows(k_b, q_b), 0.0))
        p_h[take(b), :], p_l[take(b), :] = scores_t
        local = add_rows(dot(beside(v_b), scores_t[0], TN)) + dot(v_b[0], scores_t[1], TN)
        if b:
            local = local + state_by_rows(stacked(split(before[b])), q_b)
        mine_t[:, take(b)] = local
        gg_t[:, take(b)] = jnp.transpose(g_in[take(b), :] * gains)

    for p in range(PARTS):
        s_relay(p, True)
    s_parts = []
    square, cross = [None] * blocks, [None] * blocks
    for p in range(PARTS):
        rows = pl.ds(p * (d // PARTS), d // PARTS)
        s_parts.append(s_carried(p))
        arrived = stacked(split(s_parts[p]))
        for b in range(blocks):
            mine = (mine_t[rows, take(b)] + state_by_rows(arrived, pair(q_h, q_l, b))) * scale
            mine_t[rows, take(b)] = mine
            squares = jnp.sum(mine * mine, axis=0, keepdims=True)
            crosses = jnp.sum(gg_t[rows, take(b)] * mine, axis=0, keepdims=True)
            square[b] = square[b] + squares if p else squares
            cross[b] = cross[b] + crosses if p else crosses
    s_in = jnp.concatenate(s_parts, axis=0)
    for b in range(blocks):
        for j in range(per):
            r = b * per + j
            sums[r : r + 1, :] = square[b][:, j * GROUP : (j + 1) * GROUP]
            sums[half + r : half + r + 1, :] = cross[b][:, j * GROUP : (j + 1) * GROUP]

    def partner(step):
        if n_head & (n_head - 1):
            return lax.rem(head + step, n_head)
        other, bit = head, 1
        while bit < n_head:
            if step & bit:
                other = other + bit - 2 * bit * lax.rem(head // bit, 2)
            bit *= 2
        return other

    shares = [
        pltpu.make_async_remote_copy(
            src_ref=sums, dst_ref=sums_in.at[step - 1],
            send_sem=h_send.at[step - 1], recv_sem=h_recv.at[step - 1],
            device_id={"head": partner(step)}, device_id_type=MESH,
        )
        for step in range(n_head - 1, 0, -1)
    ]
    for share in shares:
        share.start()
    total = sums[...]
    for share in shares:
        share.wait_recv()
    for step in range(1, n_head):
        total = total + sums_in[step - 1]
    features = d * n_head
    inverse = lax.rsqrt(total[:half] / features + EPS)
    factor = inverse * inverse * inverse * total[half:] / features

    def along(x, b):
        return jnp.concatenate([x[b * per + j : b * per + j + 1, :] for j in range(per)], axis=1)

    t_parts = [[] for _ in range(blocks)]
    for p in range(PARTS):
        rows = pl.ds(p * (d // PARTS), d // PARTS)
        token = lax.broadcasted_iota(jnp.int32, (d // PARTS, block), 1)
        whole = None
        for b in range(blocks):
            inv, fac = along(inverse, b), along(factor, b)
            grad = (gg_t[rows, take(b)] * inv - mine_t[rows, take(b)] * fac) * scale
            grad = split(jnp.where(token + b * block < live, grad, 0.0))
            o_h[rows, take(b)], o_l[rows, take(b)] = grad
            both = dot(jnp.concatenate(grad, axis=0), beside(pair(q_h, q_l, b)), NN)
            t_parts[b].append(add_rows(add_columns(both)))
            whole = t_parts[b][p] if whole is None else whole + t_parts[b][p]
        send_t[rows, :] = whole
        t_last(p)
    t_next()
    t_states = [jnp.concatenate(parts, axis=0) for parts in t_parts]
    after = [jnp.zeros((d, d), F32)]
    for b in range(blocks - 1, -1, -1):
        after.append(after[-1] + t_states[b])
    after = after[::-1]

    for b in range(blocks):
        q_b, k_b, v_b = pair(q_h, q_l, b), pair(k_h, k_l, b), pair(v_h, v_l, b)
        o_t = o_h[:, take(b)], o_l[:, take(b)]
        o_b = jnp.transpose(o_t[0]), jnp.transpose(o_t[1])
        normed[take(b), :] = jnp.transpose(mine_t[:, take(b)] * along(inverse, b)) * gains
        pulled_t = split(jnp.where(upper, rows_by_columns(v_b, o_t), 0.0))
        gq[take(b), :] = times_state(o_b, split(s_in + before[b])) + columns_times(pulled_t, k_b)
        later = split(after[b + 1])
        gk[take(b), :] = times(pulled_t, q_b) + times_state(v_b, later)
        gv[take(b), :] = times(pair(p_h, p_l, b), o_b) + times_state_t(k_b, later)
        if b == 1:
            for p in range(PARTS):
                t_relay(p, second)

    s_close()
    for share in shares:
        share.wait_send()
    for p in range(PARTS):
        t_relay(p, jnp.logical_not(second))
        t_out[pl.ds(p * (d // PARTS), d // PARTS), :] = t_carried(p)
    t_close()


def finish(
    block, normed, gq, gk, gv, k_h, k_l, v_h, v_l, t_in,
    normed_hbm, gq_hbm, gk_hbm, gv_hbm, gk_all, gv_all, sem,
):
    blocks = gk.shape[0] // block
    stores = [
        pltpu.make_async_copy(normed, normed_hbm, sem.at[2 * blocks]),
        pltpu.make_async_copy(gq, gq_hbm, sem.at[2 * blocks + 1]),
    ]
    for store in stores:
        store.start()
    state = split(t_in[...])

    def save(src, dst, b, i):
        rows = pl.ds(b * block, block)
        store = pltpu.make_async_copy(src.at[rows, :], dst.at[rows, :], sem.at[2 * b + i])
        store.start()
        stores.append(store)

    for b in range(blocks):
        rows = pl.ds(b * block, block)
        gk_all[rows, :] = gk[rows, :] + times_state((v_h[rows, :], v_l[rows, :]), state)
        save(gk_all, gk_hbm, b, 0)
    for b in range(blocks):
        rows = pl.ds(b * block, block)
        gv_all[rows, :] = gv[rows, :] + times_state_t((k_h[rows, :], k_l[rows, :]), state)
        save(gv_all, gv_hbm, b, 1)
    for store in stores:
        store.wait()


def on_device(n_seq, n_head, query, key_in, value, out_grad, head_scale, norm_gain, group_counts):
    cap, d = query.shape
    block = 2 * GROUP if cap % (2 * GROUP) == 0 else GROUP
    half = cap // GROUP
    blocks = cap // block
    hbm = pl.BlockSpec(memory_space=pltpu.HBM)
    vmem = pl.BlockSpec(memory_space=pltpu.VMEM)
    wide = pltpu.VMEM((cap, d), F32)
    narrow = pltpu.VMEM((cap, d), BF16)
    state = pltpu.VMEM((d, d), F32)
    states = pltpu.VMEM((n_seq - 1, d, d), F32)
    rows = jax.ShapeDtypeStruct((cap, d), F32)
    rows_low = jax.ShapeDtypeStruct((cap, d), BF16)
    held = pl.pallas_call(
        functools.partial(kernel, n_seq, n_head, block),
        out_shape=[rows] * 4 + [rows_low] * 4 + [jax.ShapeDtypeStruct((d, d), F32)],
        in_specs=[pl.BlockSpec(memory_space=pltpu.SMEM)] + [hbm] * 6,
        out_specs=[vmem] * 9,
        scratch_shapes=[pltpu.SMEM(group_counts.shape, jnp.int32)]
        + [wide] * 4 + [pltpu.VMEM((d,), F32)]
        + [narrow] * 2 + [pltpu.VMEM((cap, block), BF16)] * 2
        + [pltpu.VMEM((d, cap), F32)] * 2 + [pltpu.VMEM((d, cap), BF16)] * 2
        + [state, state, state, states] * 2
        + [pltpu.VMEM((2 * half, GROUP), F32), pltpu.VMEM((n_head - 1, 2 * half, GROUP), F32)]
        + [pltpu.SemaphoreType.DMA((6,))]
        + [pltpu.SemaphoreType.DMA((n_head - 1,))] * 2
        + [
            pltpu.SemaphoreType.DMA((PARTS,)), pltpu.SemaphoreType.DMA((n_seq - 1, PARTS)),
            pltpu.SemaphoreType.DMA((CHUNKS,)), pltpu.SemaphoreType.DMA((CHUNKS,)),
        ] * 2,
        compiler_params=pltpu.CompilerParams(
            collective_id=0, has_side_effects=True, vmem_limit_bytes=32 * 1024 * 1024
        ),
    )(head_scale, *(
        pltpu.with_memory_space_constraint(x, pltpu.HBM)
        for x in (group_counts, query, key_in, value, out_grad, norm_gain)
    ))
    return pl.pallas_call(
        functools.partial(finish, block),
        out_shape=[rows] * 4,
        in_specs=[vmem] * 9,
        out_specs=[hbm] * 4,
        scratch_shapes=[wide] * 2 + [pltpu.SemaphoreType.DMA((2 * blocks + 2,))],
        compiler_params=pltpu.CompilerParams(vmem_limit_bytes=32 * 1024 * 1024),
    )(*held)


def solution(mesh):
    rows = P("seq", "head")
    return jax.shard_map(
        functools.partial(on_device, mesh.shape["seq"], mesh.shape["head"]),
        mesh=mesh,
        in_specs=(rows, rows, rows, rows, P("head"), P("head"), P()),
        out_specs=(rows, rows, rows, rows),
        check_vma=False,
    )
```

```python
import functools

import jax
import jax.numpy as jnp
from jax import lax
from jax.experimental import pallas as pl
from jax.experimental.pallas import tpu as pltpu
from jax.sharding import PartitionSpec as P

GROUP = 128
CHUNKS = 2
PARTS = 2
EPS = 1e-05
F32 = jnp.float32
BF16 = jnp.bfloat16
MESH = pl.DeviceIdType.MESH
NN = (((1,), (0,)), ((), ()))
NT = (((1,), (1,)), ((), ()))
TN = (((0,), (0,)), ((), ()))


def dot(left, right, dims):
    return lax.dot_general(left, right, dims, preferred_element_type=F32)


def split(x):
    high = x.astype(BF16)
    low = (x - high.astype(F32)).astype(BF16)
    return high, low


def beside(pair):
    return jnp.concatenate(pair, axis=1)


def add_rows(x):
    half = x.shape[0] // 2
    return x[:half] + x[half:]


def add_columns(x):
    half = x.shape[1] // 2
    return x[:, :half] + x[:, half:]


def stacked(s):
    top = jnp.concatenate([s[0], s[0]], axis=1)
    bottom = jnp.concatenate([s[1], jnp.zeros_like(s[1])], axis=1)
    return jnp.concatenate([top, bottom], axis=0)


def rows_by_rows(a, b):
    left = jnp.concatenate([a[0], a[1], a[0]], axis=1)
    right = jnp.concatenate([b[0], b[0], b[1]], axis=1)
    return dot(left, right, NT)


def rows_by_columns(a, b):
    left = jnp.concatenate([a[0], a[1], a[0]], axis=1)
    right = jnp.concatenate([b[0], b[0], b[1]], axis=0)
    return dot(left, right, NN)


def times(a, b):
    return add_columns(dot(a[0], beside(b), NN)) + dot(a[1], b[0], NN)


def columns_times(a, b):
    return add_columns(dot(a[0], beside(b), TN)) + dot(a[1], b[0], TN)


def times_state(a, s):
    top = jnp.concatenate([s[0], s[1]], axis=1)
    bottom = jnp.concatenate([s[0], jnp.zeros_like(s[0])], axis=1)
    return add_columns(dot(beside(a), jnp.concatenate([top, bottom], axis=0), NN))


def times_state_t(a, s):
    return add_columns(dot(beside(a), stacked(s), NT))


def state_by_rows(s, a):
    return add_rows(dot(s, beside(a), NT))


def outer(a, b):
    return add_rows(add_columns(dot(beside(a), beside(b), TN)))


def kernel(
    n_seq, n_head, block, head_scale, counts_hbm,
    q_hbm, k_hbm, v_hbm, g_hbm, gain_hbm,
    normed, gq, gk, gv, k_h, k_l, v_h, v_l, t_out,
    counts, q_in, k_in, v_in, g_in, gain,
    q_h, q_l, p_h, p_l, mine_t, gg_t, o_h, o_l,
    send_s, pass_s, near_s, far_s, send_t, pass_t, near_t, far_t, sums, sums_in,
    in_sem, h_send, h_recv, *seq_sems,
):
    cap, d = q_in.shape
    blocks = cap // block
    per = block // GROUP
    pos = lax.axis_index("seq")
    head = lax.axis_index("head")
    half = sums.shape[0] // 2
    second = lax.rem(head, 2) == 1

    s_sems, t_sems = seq_sems[:4], seq_sems[4:]

    barrier = pltpu.get_barrier_semaphore()
    last = n_seq - 1
    direct = n_seq <= 4
    merge = direct and last == 3
    own_way = jnp.logical_not(second) if merge else True
    ahead = not merge

    def both(a, b):
        return jnp.logical_and(a, b)

    def sends(source, target):
        to_next = both(target == source + 1, target < last if direct else True)
        to_next_back = both(target == source - 1, target > 0 if direct else True)
        near = jnp.logical_or(to_next, to_next_back)
        if not direct:
            return near
        to_end = both(target == last, both(source < last, jnp.logical_or(source > 0, ahead)))
        to_start = both(target == 0, both(source > 0, jnp.logical_or(source < last, own_way)))
        return jnp.logical_or(near, jnp.logical_or(to_end, to_start))

    for other in range(n_seq):

        @pl.when(sends(other, pos))
        def _():
            pl.semaphore_signal(barrier, inc=1, device_id={"seq": other}, device_id_type=MESH)

    loads = [
        pltpu.make_async_copy(src, dst, in_sem.at[i])
        for i, (src, dst) in enumerate(
            (
                (counts_hbm, counts), (k_hbm, k_in), (v_hbm, v_in), (q_hbm, q_in),
                (g_hbm, g_in), (gain_hbm, gain),
            )
        )
    ]
    for load in loads:
        load.start()
    for step in range(1, n_head):
        pl.semaphore_signal(barrier, inc=1, device_id={"head": lax.rem(head + step, n_head)}, device_id_type=MESH)

    def exchange(way, src, passed, near, far, sems):
        far_send, far_recv, near_send, near_recv = sems
        order = pos if way == 1 else n_seq - 1 - pos
        middle = jnp.logical_and(order > 0, order < (last - 1 if direct else last))
        heads_chain = jnp.logical_and(order == 0, last > (1 if direct else 0))

        skips = True if way == 1 else second
        merged = jnp.logical_and(skips, order <= 1) if merge else False

        def piece(p, parts):
            return pl.ds(p * (d // parts), d // parts)

        def far_copy(k, p, source=src):
            return pltpu.make_async_remote_copy(
                src_ref=source.at[piece(p, PARTS), :], dst_ref=far.at[k, piece(p, PARTS), :],
                send_sem=far_send.at[p], recv_sem=far_recv.at[k, p],
                device_id={"seq": last if way == 1 else 0}, device_id_type=MESH,
            )

        def to_next(source, c):
            rows = piece(c, CHUNKS)
            return pltpu.make_async_remote_copy(
                src_ref=source.at[rows, :], dst_ref=near.at[rows, :],
                send_sem=near_send.at[c], recv_sem=near_recv.at[c],
                device_id={"seq": pos + way}, device_id_type=MESH,
            )

        def clear():
            @pl.when(jnp.logical_or(order == 0, order == last) if direct else order == 0)
            def _():
                near[...] = jnp.zeros_like(near)

            if direct:

                @pl.when(order < last)
                def _():
                    far[...] = jnp.zeros_like(far)

                if merge:

                    @pl.when(jnp.logical_and(order == last, skips))
                    def _():
                        far[0] = jnp.zeros(far.shape[1:], F32)

        def start_last(p):
            if direct:

                @pl.when(jnp.logical_and(order < last, jnp.logical_not(merged)))
                def _():
                    far_copy(order, p).start()

        def start_next():
            @pl.when(heads_chain)
            def _():
                for c in range(CHUNKS):
                    to_next(src, c).start()

        def relay(p, when):
            chunks = range(p * (CHUNKS // PARTS), (p + 1) * (CHUNKS // PARTS))

            def pass_on():
                for c in chunks:
                    to_next(passed, c).start()

            @pl.when(jnp.logical_and(middle, when))
            def _():
                for c in chunks:
                    rows = piece(c, CHUNKS)
                    to_next(src, c).wait_recv()
                    passed[rows, :] = src[rows, :] + near[rows, :]
                    if not merge:
                        to_next(passed, c).start()

                if merge:

                    @pl.when(merged)
                    def _():
                        far_copy(1, p, passed).start()

                        if p == PARTS - 1:
                            for c in range(CHUNKS):
                                to_next(passed, c).start()

                    @pl.when(jnp.logical_not(merged))
                    def _():
                        pass_on()

        def carried(p):
            per_part = CHUNKS // PARTS

            if not direct or last > 1:

                @pl.when(order == (last - 1 if direct else last))
                def _():
                    for c in range(p * per_part, (p + 1) * per_part):
                        to_next(src, c).wait_recv()

            if direct:

                @pl.when(order == last)
                def _():
                    for k in range(1 if merge else 0, last):
                        far_copy(k, p).wait_recv()

                if merge and way == -1:

                    @pl.when(jnp.logical_and(order == last, jnp.logical_not(second)))
                    def _():
                        far_copy(0, p).wait_recv()

            total = near[piece(p, PARTS), :]
            if direct:
                for k in range(last):
                    total = total + far[k, piece(p, PARTS), :]
            return total

        def close():
            if direct:

                @pl.when(jnp.logical_and(order < last, jnp.logical_or(order > 0, jnp.logical_not(merged))))
                def _():
                    for p in range(PARTS):
                        far_copy(order, p).wait_send()

            @pl.when(jnp.logical_or(heads_chain, middle))
            def _():
                for c in range(CHUNKS):
                    to_next(src, c).wait_send()

        return clear, start_last, start_next, relay, carried, close

    s_clear, s_last, s_next, s_relay, s_carried, s_close = exchange(1, send_s, pass_s, near_s, far_s, s_sems)
    t_clear, t_last, t_next, t_relay, t_carried, t_close = exchange(-1, send_t, pass_t, near_t, far_t, t_sems)
    s_clear()
    t_clear()

    row = lax.broadcasted_iota(jnp.int32, (block, d), 0)
    upper = lax.broadcasted_iota(jnp.int32, (block, block), 0) <= lax.broadcasted_iota(jnp.int32, (block, block), 1)

    def take(b):
        return pl.ds(b * block, block)

    def pair(high, low, b):
        return high[take(b), :], low[take(b), :]

    loads[0].wait()
    live = counts[pos] * GROUP

    def keep(source, high, low, b):
        x = jnp.where(row + b * block < live, source[take(b), :], 0.0)
        high[take(b), :], low[take(b), :] = split(x)

    loads[1].wait()
    loads[2].wait()
    before = [jnp.zeros((d, d), F32)]
    for b in range(blocks):
        keep(k_in, k_h, k_l, b)
        keep(v_in, v_h, v_l, b)
        before.append(before[-1] + outer(pair(v_h, v_l, b), pair(k_h, k_l, b)))
    send_s[...] = before[-1]
    greeted = n_head - 1
    for other in range(n_seq):
        greeted = greeted + jnp.where(sends(pos, other), 1, 0)
    pl.semaphore_wait(barrier, greeted)
    s_next()
    for p in range(PARTS):
        s_last(p)

    loads[3].wait()
    loads[4].wait()
    loads[5].wait()
    scale = head_scale[0]
    gains = gain[...].reshape(1, d)
    for b in range(blocks):
        keep(q_in, q_h, q_l, b)
        q_b, k_b, v_b = pair(q_h, q_l, b), pair(k_h, k_l, b), pair(v_h, v_l, b)
        scores_t = split(jnp.where(upper, rows_by_rows(k_b, q_b), 0.0))
        p_h[take(b), :], p_l[take(b), :] = scores_t
        local = add_rows(dot(beside(v_b), scores_t[0], TN)) + dot(v_b[0], scores_t[1], TN)
        if b:
            local = local + state_by_rows(stacked(split(before[b])), q_b)
        mine_t[:, take(b)] = local
        gg_t[:, take(b)] = jnp.transpose(g_in[take(b), :] * gains)

    for p in range(PARTS):
        s_relay(p, True)
    s_parts = []
    square, cross = [None] * blocks, [None] * blocks
    for p in range(PARTS):
        rows = pl.ds(p * (d // PARTS), d // PARTS)
        s_parts.append(s_carried(p))
        arrived = stacked(split(s_parts[p]))
        for b in range(blocks):
            mine = (mine_t[rows, take(b)] + state_by_rows(arrived, pair(q_h, q_l, b))) * scale
            mine_t[rows, take(b)] = mine
            squares = jnp.sum(mine * mine, axis=0, keepdims=True)
            crosses = jnp.sum(gg_t[rows, take(b)] * mine, axis=0, keepdims=True)
            square[b] = square[b] + squares if p else squares
            cross[b] = cross[b] + crosses if p else crosses
    s_in = jnp.concatenate(s_parts, axis=0)
    for b in range(blocks):
        for j in range(per):
            r = b * per + j
            sums[r : r + 1, :] = square[b][:, j * GROUP : (j + 1) * GROUP]
            sums[half + r : half + r + 1, :] = cross[b][:, j * GROUP : (j + 1) * GROUP]

    def partner(step):
        if n_head & (n_head - 1):
            return lax.rem(head + step, n_head)
        other, bit = head, 1
        while bit < n_head:
            if step & bit:
                other = other + bit - 2 * bit * lax.rem(head // bit, 2)
            bit *= 2
        return other

    shares = [
        pltpu.make_async_remote_copy(
            src_ref=sums, dst_ref=sums_in.at[step - 1],
            send_sem=h_send.at[step - 1], recv_sem=h_recv.at[step - 1],
            device_id={"head": partner(step)}, device_id_type=MESH,
        )
        for step in range(n_head - 1, 0, -1)
    ]
    for share in shares:
        share.start()
    total = sums[...]
    for share in shares:
        share.wait_recv()
    for step in range(1, n_head):
        total = total + sums_in[step - 1]
    features = d * n_head
    inverse = lax.rsqrt(total[:half] / features + EPS)
    factor = inverse * inverse * inverse * total[half:] / features

    def along(x, b):
        return jnp.concatenate([x[b * per + j : b * per + j + 1, :] for j in range(per)], axis=1)

    t_parts = [[] for _ in range(blocks)]
    for p in range(PARTS):
        rows = pl.ds(p * (d // PARTS), d // PARTS)
        token = lax.broadcasted_iota(jnp.int32, (d // PARTS, block), 1)
        whole = None
        for b in range(blocks):
            inv, fac = along(inverse, b), along(factor, b)
            grad = (gg_t[rows, take(b)] * inv - mine_t[rows, take(b)] * fac) * scale
            grad = split(jnp.where(token + b * block < live, grad, 0.0))
            o_h[rows, take(b)], o_l[rows, take(b)] = grad
            both = dot(jnp.concatenate(grad, axis=0), beside(pair(q_h, q_l, b)), NN)
            t_parts[b].append(add_rows(add_columns(both)))
            whole = t_parts[b][p] if whole is None else whole + t_parts[b][p]
        send_t[rows, :] = whole
        t_last(p)
    t_next()
    t_states = [jnp.concatenate(parts, axis=0) for parts in t_parts]
    after = [jnp.zeros((d, d), F32)]
    for b in range(blocks - 1, -1, -1):
        after.append(after[-1] + t_states[b])
    after = after[::-1]

    for b in range(blocks):
        q_b, k_b, v_b = pair(q_h, q_l, b), pair(k_h, k_l, b), pair(v_h, v_l, b)
        o_t = o_h[:, take(b)], o_l[:, take(b)]
        o_b = jnp.transpose(o_t[0]), jnp.transpose(o_t[1])
        normed[take(b), :] = jnp.transpose(mine_t[:, take(b)] * along(inverse, b)) * gains
        pulled_t = split(jnp.where(upper, rows_by_columns(v_b, o_t), 0.0))
        gq[take(b), :] = times_state(o_b, split(s_in + before[b])) + columns_times(pulled_t, k_b)
        later = split(after[b + 1])
        gk[take(b), :] = times(pulled_t, q_b) + times_state(v_b, later)
        gv[take(b), :] = times(pair(p_h, p_l, b), o_b) + times_state_t(k_b, later)
        if b == 1:
            for p in range(PARTS):
                t_relay(p, second)

    s_close()
    for share in shares:
        share.wait_send()
    for p in range(PARTS):
        t_relay(p, jnp.logical_not(second))
        t_out[pl.ds(p * (d // PARTS), d // PARTS), :] = t_carried(p)
    t_close()


def finish(
    block, normed, gq, gk, gv, k_h, k_l, v_h, v_l, t_in,
    normed_hbm, gq_hbm, gk_hbm, gv_hbm, gk_all, gv_all, sem,
):
    blocks = gk.shape[0] // block
    stores = [
        pltpu.make_async_copy(normed, normed_hbm, sem.at[2 * blocks]),
        pltpu.make_async_copy(gq, gq_hbm, sem.at[2 * blocks + 1]),
    ]
    for store in stores:
        store.start()
    state = split(t_in[...])

    def save(src, dst, b, i):
        rows = pl.ds(b * block, block)
        store = pltpu.make_async_copy(src.at[rows, :], dst.at[rows, :], sem.at[2 * b + i])
        store.start()
        stores.append(store)

    for b in range(blocks):
        rows = pl.ds(b * block, block)
        gk_all[rows, :] = gk[rows, :] + times_state((v_h[rows, :], v_l[rows, :]), state)
        save(gk_all, gk_hbm, b, 0)
    for b in range(blocks):
        rows = pl.ds(b * block, block)
        gv_all[rows, :] = gv[rows, :] + times_state_t((k_h[rows, :], k_l[rows, :]), state)
        save(gv_all, gv_hbm, b, 1)
    for store in stores:
        store.wait()


def on_device(n_seq, n_head, query, key_in, value, out_grad, head_scale, norm_gain, group_counts):
    cap, d = query.shape
    block = 2 * GROUP if cap % (2 * GROUP) == 0 else GROUP
    half = cap // GROUP
    blocks = cap // block
    hbm = pl.BlockSpec(memory_space=pltpu.HBM)
    vmem = pl.BlockSpec(memory_space=pltpu.VMEM)
    wide = pltpu.VMEM((cap, d), F32)
    narrow = pltpu.VMEM((cap, d), BF16)
    state = pltpu.VMEM((d, d), F32)
    states = pltpu.VMEM((n_seq - 1, d, d), F32)
    rows = jax.ShapeDtypeStruct((cap, d), F32)
    rows_low = jax.ShapeDtypeStruct((cap, d), BF16)
    held = pl.pallas_call(
        functools.partial(kernel, n_seq, n_head, block),
        out_shape=[rows] * 4 + [rows_low] * 4 + [jax.ShapeDtypeStruct((d, d), F32)],
        in_specs=[pl.BlockSpec(memory_space=pltpu.SMEM)] + [hbm] * 6,
        out_specs=[vmem] * 9,
        scratch_shapes=[pltpu.SMEM(group_counts.shape, jnp.int32)]
        + [wide] * 4 + [pltpu.VMEM((d,), F32)]
        + [narrow] * 2 + [pltpu.VMEM((cap, block), BF16)] * 2
        + [pltpu.VMEM((d, cap), F32)] * 2 + [pltpu.VMEM((d, cap), BF16)] * 2
        + [state, state, state, states] * 2
        + [pltpu.VMEM((2 * half, GROUP), F32), pltpu.VMEM((n_head - 1, 2 * half, GROUP), F32)]
        + [pltpu.SemaphoreType.DMA((6,))]
        + [pltpu.SemaphoreType.DMA((n_head - 1,))] * 2
        + [
            pltpu.SemaphoreType.DMA((PARTS,)), pltpu.SemaphoreType.DMA((n_seq - 1, PARTS)),
            pltpu.SemaphoreType.DMA((CHUNKS,)), pltpu.SemaphoreType.DMA((CHUNKS,)),
        ] * 2,
        compiler_params=pltpu.CompilerParams(
            collective_id=0, has_side_effects=True, vmem_limit_bytes=32 * 1024 * 1024
        ),
    )(head_scale, *(
        pltpu.with_memory_space_constraint(x, pltpu.HBM)
        for x in (group_counts, query, key_in, value, out_grad, norm_gain)
    ))
    return pl.pallas_call(
        functools.partial(finish, block),
        out_shape=[rows] * 4,
        in_specs=[vmem] * 9,
        out_specs=[hbm] * 4,
        scratch_shapes=[wide] * 2 + [pltpu.SemaphoreType.DMA((2 * blocks + 2,))],
        compiler_params=pltpu.CompilerParams(vmem_limit_bytes=32 * 1024 * 1024),
    )(*held)


def solution(mesh):
    rows = P("seq", "head")
    return jax.shard_map(
        functools.partial(on_device, mesh.shape["seq"], mesh.shape["head"]),
        mesh=mesh,
        in_specs=(rows, rows, rows, rows, P("head"), P("head"), P()),
        out_specs=(rows, rows, rows, rows),
        check_vma=False,
    )
```

```python
import functools

import jax
import jax.numpy as jnp
from jax import lax
from jax.experimental import pallas as pl
from jax.experimental.pallas import tpu as pltpu
from jax.sharding import PartitionSpec as P

GROUP = 128
CHUNKS = 2
PARTS = 2
EPS = 1e-05
F32 = jnp.float32
BF16 = jnp.bfloat16
MESH = pl.DeviceIdType.MESH
NN = (((1,), (0,)), ((), ()))
NT = (((1,), (1,)), ((), ()))
TN = (((0,), (0,)), ((), ()))


def dot(left, right, dims):
    return lax.dot_general(left, right, dims, preferred_element_type=F32)


def split(x):
    high = x.astype(BF16)
    low = (x - high.astype(F32)).astype(BF16)
    return high, low


def beside(pair):
    return jnp.concatenate(pair, axis=1)


def add_rows(x):
    half = x.shape[0] // 2
    return x[:half] + x[half:]


def add_columns(x):
    half = x.shape[1] // 2
    return x[:, :half] + x[:, half:]


def stacked(s):
    top = jnp.concatenate([s[0], s[0]], axis=1)
    bottom = jnp.concatenate([s[1], jnp.zeros_like(s[1])], axis=1)
    return jnp.concatenate([top, bottom], axis=0)


def rows_by_rows(a, b):
    left = jnp.concatenate([a[0], a[1], a[0]], axis=1)
    right = jnp.concatenate([b[0], b[0], b[1]], axis=1)
    return dot(left, right, NT)


def rows_by_columns(a, b):
    left = jnp.concatenate([a[0], a[1], a[0]], axis=1)
    right = jnp.concatenate([b[0], b[0], b[1]], axis=0)
    return dot(left, right, NN)


def times(a, b):
    return add_columns(dot(a[0], beside(b), NN)) + dot(a[1], b[0], NN)


def columns_times(a, b):
    return add_columns(dot(a[0], beside(b), TN)) + dot(a[1], b[0], TN)


def times_state(a, s):
    top = jnp.concatenate([s[0], s[1]], axis=1)
    bottom = jnp.concatenate([s[0], jnp.zeros_like(s[0])], axis=1)
    return add_columns(dot(beside(a), jnp.concatenate([top, bottom], axis=0), NN))


def times_state_t(a, s):
    return add_columns(dot(beside(a), stacked(s), NT))


def state_by_rows(s, a):
    return add_rows(dot(s, beside(a), NT))


def outer(a, b):
    return add_rows(add_columns(dot(beside(a), beside(b), TN)))


def kernel(
    n_seq, n_head, block, head_scale, counts_hbm,
    q_hbm, k_hbm, v_hbm, g_hbm, gain_hbm,
    normed, gq, gk, gv, k_h, k_l, v_h, v_l, t_out,
    counts, q_in, k_in, v_in, g_in, gain,
    q_h, q_l, p_h, p_l, mine_t, gg_t, o_h, o_l,
    send_s, pass_s, near_s, far_s, send_t, pass_t, near_t, far_t, sums, sums_in,
    in_sem, h_send, h_recv, *seq_sems,
):
    cap, d = q_in.shape
    blocks = cap // block
    per = block // GROUP
    pos = lax.axis_index("seq")
    head = lax.axis_index("head")
    half = sums.shape[0] // 2
    second = lax.rem(head, 2) == 1

    s_sems, t_sems = seq_sems[:4], seq_sems[4:]

    barrier = pltpu.get_barrier_semaphore()
    last = n_seq - 1
    direct = n_seq <= 4
    merge = direct and last == 3
    own_way = jnp.logical_not(second) if merge else True
    ahead = not merge

    def both(a, b):
        return jnp.logical_and(a, b)

    def sends(source, target):
        to_next = both(target == source + 1, target < last if direct else True)
        to_next_back = both(target == source - 1, target > 0 if direct else True)
        near = jnp.logical_or(to_next, to_next_back)
        if not direct:
            return near
        to_end = both(target == last, both(source < last, jnp.logical_or(source > 0, ahead)))
        to_start = both(target == 0, both(source > 0, jnp.logical_or(source < last, own_way)))
        return jnp.logical_or(near, jnp.logical_or(to_end, to_start))

    for other in range(n_seq):

        @pl.when(sends(other, pos))
        def _():
            pl.semaphore_signal(barrier, inc=1, device_id={"seq": other}, device_id_type=MESH)

    loads = [
        pltpu.make_async_copy(src, dst, in_sem.at[i])
        for i, (src, dst) in enumerate(
            (
                (counts_hbm, counts), (k_hbm, k_in), (v_hbm, v_in), (q_hbm, q_in),
                (g_hbm, g_in), (gain_hbm, gain),
            )
        )
    ]
    for load in loads:
        load.start()
    for step in range(1, n_head):
        pl.semaphore_signal(barrier, inc=1, device_id={"head": lax.rem(head + step, n_head)}, device_id_type=MESH)

    def exchange(way, src, passed, near, far, sems):
        far_send, far_recv, near_send, near_recv = sems
        order = pos if way == 1 else n_seq - 1 - pos
        middle = jnp.logical_and(order > 0, order < (last - 1 if direct else last))
        heads_chain = jnp.logical_and(order == 0, last > (1 if direct else 0))

        skips = True if way == 1 else second
        merged = jnp.logical_and(skips, order <= 1) if merge else False

        def piece(p, parts):
            return pl.ds(p * (d // parts), d // parts)

        def far_copy(k, p, source=src):
            return pltpu.make_async_remote_copy(
                src_ref=source.at[piece(p, PARTS), :], dst_ref=far.at[k, piece(p, PARTS), :],
                send_sem=far_send.at[p], recv_sem=far_recv.at[k, p],
                device_id={"seq": last if way == 1 else 0}, device_id_type=MESH,
            )

        def to_next(source, c):
            rows = piece(c, CHUNKS)
            return pltpu.make_async_remote_copy(
                src_ref=source.at[rows, :], dst_ref=near.at[rows, :],
                send_sem=near_send.at[c], recv_sem=near_recv.at[c],
                device_id={"seq": pos + way}, device_id_type=MESH,
            )

        def clear():
            @pl.when(jnp.logical_or(order == 0, order == last) if direct else order == 0)
            def _():
                near[...] = jnp.zeros_like(near)

            if direct:

                @pl.when(order < last)
                def _():
                    far[...] = jnp.zeros_like(far)

                if merge:

                    @pl.when(jnp.logical_and(order == last, skips))
                    def _():
                        far[0] = jnp.zeros(far.shape[1:], F32)

        def start_last(p):
            if direct:

                @pl.when(jnp.logical_and(order < last, jnp.logical_not(merged)))
                def _():
                    far_copy(order, p).start()

        def start_next():
            @pl.when(heads_chain)
            def _():
                for c in range(CHUNKS):
                    to_next(src, c).start()

        def relay(p, when):
            chunks = range(p * (CHUNKS // PARTS), (p + 1) * (CHUNKS // PARTS))

            def pass_on():
                for c in chunks:
                    to_next(passed, c).start()

            @pl.when(jnp.logical_and(middle, when))
            def _():
                for c in chunks:
                    rows = piece(c, CHUNKS)
                    to_next(src, c).wait_recv()
                    passed[rows, :] = src[rows, :] + near[rows, :]
                    if not merge:
                        to_next(passed, c).start()

                if merge:

                    @pl.when(merged)
                    def _():
                        far_copy(1, p, passed).start()

                        if p == PARTS - 1:
                            for c in range(CHUNKS):
                                to_next(passed, c).start()

                    @pl.when(jnp.logical_not(merged))
                    def _():
                        pass_on()

        def carried(p):
            per_part = CHUNKS // PARTS

            if not direct or last > 1:

                @pl.when(order == (last - 1 if direct else last))
                def _():
                    for c in range(p * per_part, (p + 1) * per_part):
                        to_next(src, c).wait_recv()

            if direct:

                @pl.when(order == last)
                def _():
                    for k in range(1 if merge else 0, last):
                        far_copy(k, p).wait_recv()

                if merge and way == -1:

                    @pl.when(jnp.logical_and(order == last, jnp.logical_not(second)))
                    def _():
                        far_copy(0, p).wait_recv()

            total = near[piece(p, PARTS), :]
            if direct:
                for k in range(last):
                    total = total + far[k, piece(p, PARTS), :]
            return total

        def close():
            if direct:

                @pl.when(jnp.logical_and(order < last, jnp.logical_or(order > 0, jnp.logical_not(merged))))
                def _():
                    for p in range(PARTS):
                        far_copy(order, p).wait_send()

            @pl.when(jnp.logical_or(heads_chain, middle))
            def _():
                for c in range(CHUNKS):
                    to_next(src, c).wait_send()

        return clear, start_last, start_next, relay, carried, close

    s_clear, s_last, s_next, s_relay, s_carried, s_close = exchange(1, send_s, pass_s, near_s, far_s, s_sems)
    t_clear, t_last, t_next, t_relay, t_carried, t_close = exchange(-1, send_t, pass_t, near_t, far_t, t_sems)
    s_clear()
    t_clear()

    row = lax.broadcasted_iota(jnp.int32, (block, d), 0)
    upper = lax.broadcasted_iota(jnp.int32, (block, block), 0) <= lax.broadcasted_iota(jnp.int32, (block, block), 1)

    def take(b):
        return pl.ds(b * block, block)

    def pair(high, low, b):
        return high[take(b), :], low[take(b), :]

    loads[0].wait()
    live = counts[pos] * GROUP

    def keep(source, high, low, b):
        x = jnp.where(row + b * block < live, source[take(b), :], 0.0)
        high[take(b), :], low[take(b), :] = split(x)

    loads[1].wait()
    loads[2].wait()
    before = [jnp.zeros((d, d), F32)]
    for b in range(blocks):
        keep(k_in, k_h, k_l, b)
        keep(v_in, v_h, v_l, b)
        before.append(before[-1] + outer(pair(v_h, v_l, b), pair(k_h, k_l, b)))
    send_s[...] = before[-1]
    greeted = n_head - 1
    for other in range(n_seq):
        greeted = greeted + jnp.where(sends(pos, other), 1, 0)
    pl.semaphore_wait(barrier, greeted)
    s_next()
    for p in range(PARTS):
        s_last(p)

    loads[3].wait()
    loads[4].wait()
    loads[5].wait()
    scale = head_scale[0]
    gains = gain[...].reshape(1, d)
    for b in range(blocks):
        keep(q_in, q_h, q_l, b)
        q_b, k_b, v_b = pair(q_h, q_l, b), pair(k_h, k_l, b), pair(v_h, v_l, b)
        scores_t = split(jnp.where(upper, rows_by_rows(k_b, q_b), 0.0))
        p_h[take(b), :], p_l[take(b), :] = scores_t
        local = add_rows(dot(beside(v_b), scores_t[0], TN)) + dot(v_b[0], scores_t[1], TN)
        if b:
            local = local + state_by_rows(stacked(split(before[b])), q_b)
        mine_t[:, take(b)] = local
        gg_t[:, take(b)] = jnp.transpose(g_in[take(b), :] * gains)

    for p in range(PARTS):
        s_relay(p, True)
    s_parts = []
    square, cross = [None] * blocks, [None] * blocks
    for p in range(PARTS):
        rows = pl.ds(p * (d // PARTS), d // PARTS)
        s_parts.append(s_carried(p))
        arrived = stacked(split(s_parts[p]))
        for b in range(blocks):
            mine = (mine_t[rows, take(b)] + state_by_rows(arrived, pair(q_h, q_l, b))) * scale
            mine_t[rows, take(b)] = mine
            squares = jnp.sum(mine * mine, axis=0, keepdims=True)
            crosses = jnp.sum(gg_t[rows, take(b)] * mine, axis=0, keepdims=True)
            square[b] = square[b] + squares if p else squares
            cross[b] = cross[b] + crosses if p else crosses
    s_in = jnp.concatenate(s_parts, axis=0)
    for b in range(blocks):
        for j in range(per):
            r = b * per + j
            sums[r : r + 1, :] = square[b][:, j * GROUP : (j + 1) * GROUP]
            sums[half + r : half + r + 1, :] = cross[b][:, j * GROUP : (j + 1) * GROUP]

    def partner(step):
        if n_head & (n_head - 1):
            return lax.rem(head + step, n_head)
        other, bit = head, 1
        while bit < n_head:
            if step & bit:
                other = other + bit - 2 * bit * lax.rem(head // bit, 2)
            bit *= 2
        return other

    shares = [
        pltpu.make_async_remote_copy(
            src_ref=sums, dst_ref=sums_in.at[step - 1],
            send_sem=h_send.at[step - 1], recv_sem=h_recv.at[step - 1],
            device_id={"head": partner(step)}, device_id_type=MESH,
        )
        for step in range(n_head - 1, 0, -1)
    ]
    for share in shares:
        share.start()
    total = sums[...]
    for share in shares:
        share.wait_recv()
    for step in range(1, n_head):
        total = total + sums_in[step - 1]
    features = d * n_head
    inverse = lax.rsqrt(total[:half] / features + EPS)
    factor = inverse * inverse * inverse * total[half:] / features

    def along(x, b):
        return jnp.concatenate([x[b * per + j : b * per + j + 1, :] for j in range(per)], axis=1)

    t_parts = [[] for _ in range(blocks)]
    for p in range(PARTS):
        rows = pl.ds(p * (d // PARTS), d // PARTS)
        token = lax.broadcasted_iota(jnp.int32, (d // PARTS, block), 1)
        whole = None
        for b in range(blocks):
            inv, fac = along(inverse, b), along(factor, b)
            grad = (gg_t[rows, take(b)] * inv - mine_t[rows, take(b)] * fac) * scale
            grad = split(jnp.where(token + b * block < live, grad, 0.0))
            o_h[rows, take(b)], o_l[rows, take(b)] = grad
            both = dot(jnp.concatenate(grad, axis=0), beside(pair(q_h, q_l, b)), NN)
            t_parts[b].append(add_rows(add_columns(both)))
            whole = t_parts[b][p] if whole is None else whole + t_parts[b][p]
        send_t[rows, :] = whole
        t_last(p)
    t_next()
    t_states = [jnp.concatenate(parts, axis=0) for parts in t_parts]
    after = [jnp.zeros((d, d), F32)]
    for b in range(blocks - 1, -1, -1):
        after.append(after[-1] + t_states[b])
    after = after[::-1]

    for b in range(blocks):
        q_b, k_b, v_b = pair(q_h, q_l, b), pair(k_h, k_l, b), pair(v_h, v_l, b)
        o_t = o_h[:, take(b)], o_l[:, take(b)]
        o_b = jnp.transpose(o_t[0]), jnp.transpose(o_t[1])
        normed[take(b), :] = jnp.transpose(mine_t[:, take(b)] * along(inverse, b)) * gains
        pulled_t = split(jnp.where(upper, rows_by_columns(v_b, o_t), 0.0))
        gq[take(b), :] = times_state(o_b, split(s_in + before[b])) + columns_times(pulled_t, k_b)
        later = split(after[b + 1])
        gk[take(b), :] = times(pulled_t, q_b) + times_state(v_b, later)
        gv[take(b), :] = times(pair(p_h, p_l, b), o_b) + times_state_t(k_b, later)
        if b == min(1, blocks - 1):
            for p in range(PARTS):
                t_relay(p, second)

    s_close()
    for share in shares:
        share.wait_send()
    for p in range(PARTS):
        t_relay(p, jnp.logical_not(second))
        t_out[pl.ds(p * (d // PARTS), d // PARTS), :] = t_carried(p)
    t_close()


def finish(
    block, normed, gq, gk, gv, k_h, k_l, v_h, v_l, t_in,
    normed_hbm, gq_hbm, gk_hbm, gv_hbm, gk_all, gv_all, sem,
):
    blocks = gk.shape[0] // block
    stores = [
        pltpu.make_async_copy(normed, normed_hbm, sem.at[2 * blocks]),
        pltpu.make_async_copy(gq, gq_hbm, sem.at[2 * blocks + 1]),
    ]
    for store in stores:
        store.start()
    state = split(t_in[...])

    def save(src, dst, b, i):
        rows = pl.ds(b * block, block)
        store = pltpu.make_async_copy(src.at[rows, :], dst.at[rows, :], sem.at[2 * b + i])
        store.start()
        stores.append(store)

    for b in range(blocks):
        rows = pl.ds(b * block, block)
        gk_all[rows, :] = gk[rows, :] + times_state((v_h[rows, :], v_l[rows, :]), state)
        save(gk_all, gk_hbm, b, 0)
    for b in range(blocks):
        rows = pl.ds(b * block, block)
        gv_all[rows, :] = gv[rows, :] + times_state_t((k_h[rows, :], k_l[rows, :]), state)
        save(gv_all, gv_hbm, b, 1)
    for store in stores:
        store.wait()


def on_device(n_seq, n_head, query, key_in, value, out_grad, head_scale, norm_gain, group_counts):
    cap, d = query.shape
    block = 2 * GROUP if cap % (2 * GROUP) == 0 else GROUP
    half = cap // GROUP
    blocks = cap // block
    hbm = pl.BlockSpec(memory_space=pltpu.HBM)
    vmem = pl.BlockSpec(memory_space=pltpu.VMEM)
    wide = pltpu.VMEM((cap, d), F32)
    narrow = pltpu.VMEM((cap, d), BF16)
    state = pltpu.VMEM((d, d), F32)
    states = pltpu.VMEM((n_seq - 1, d, d), F32)
    rows = jax.ShapeDtypeStruct((cap, d), F32)
    rows_low = jax.ShapeDtypeStruct((cap, d), BF16)
    held = pl.pallas_call(
        functools.partial(kernel, n_seq, n_head, block),
        out_shape=[rows] * 4 + [rows_low] * 4 + [jax.ShapeDtypeStruct((d, d), F32)],
        in_specs=[pl.BlockSpec(memory_space=pltpu.SMEM)] + [hbm] * 6,
        out_specs=[vmem] * 9,
        scratch_shapes=[pltpu.SMEM(group_counts.shape, jnp.int32)]
        + [wide] * 4 + [pltpu.VMEM((d,), F32)]
        + [narrow] * 2 + [pltpu.VMEM((cap, block), BF16)] * 2
        + [pltpu.VMEM((d, cap), F32)] * 2 + [pltpu.VMEM((d, cap), BF16)] * 2
        + [state, state, state, states] * 2
        + [pltpu.VMEM((2 * half, GROUP), F32), pltpu.VMEM((n_head - 1, 2 * half, GROUP), F32)]
        + [pltpu.SemaphoreType.DMA((6,))]
        + [pltpu.SemaphoreType.DMA((n_head - 1,))] * 2
        + [
            pltpu.SemaphoreType.DMA((PARTS,)), pltpu.SemaphoreType.DMA((n_seq - 1, PARTS)),
            pltpu.SemaphoreType.DMA((CHUNKS,)), pltpu.SemaphoreType.DMA((CHUNKS,)),
        ] * 2,
        compiler_params=pltpu.CompilerParams(
            collective_id=0, has_side_effects=True, vmem_limit_bytes=32 * 1024 * 1024
        ),
    )(head_scale, *(
        pltpu.with_memory_space_constraint(x, pltpu.HBM)
        for x in (group_counts, query, key_in, value, out_grad, norm_gain)
    ))
    return pl.pallas_call(
        functools.partial(finish, block),
        out_shape=[rows] * 4,
        in_specs=[vmem] * 9,
        out_specs=[hbm] * 4,
        scratch_shapes=[wide] * 2 + [pltpu.SemaphoreType.DMA((2 * blocks + 2,))],
        compiler_params=pltpu.CompilerParams(vmem_limit_bytes=32 * 1024 * 1024),
    )(*held)


def solution(mesh):
    rows = P("seq", "head")
    return jax.shard_map(
        functools.partial(on_device, mesh.shape["seq"], mesh.shape["head"]),
        mesh=mesh,
        in_specs=(rows, rows, rows, rows, P("head"), P("head"), P()),
        out_specs=(rows, rows, rows, rows),
        check_vma=False,
    )
```
